256 devices in a mesh: pipe: 4 (over y), seq: 64 (over x, z, core).
Axes of the slice: x: 4, y: 4, z: 8, core: 2. Of those that a mesh axis runs over, the one named last changes fastest.
Arguments:
- in_flight: bfloat16 [4, 65536, 1024], P('pipe', 'seq'), may hold values from -6 to 6
- fresh_rows: bfloat16 [65536, 1024], P('seq'), may hold values from -6 to 6
- right_factor: bfloat16 [4, 256, 256, 256], P('pipe', 'seq'), may hold values from -0.375 to 0.375
- left_factor: bfloat16 [4, 256, 256, 256], P('pipe', 'seq'), may hold values from -0.375 to 0.375
- gate_gain: float32 [4, 1024], P('pipe'), may hold values from -4 to 4
- gate_bias: float32 [4, 1024], P('pipe'), may hold values from -4 to 4
- norm_gain: float32 [4, 1024], P('pipe'), may hold values from 0.5 to 1.5
- w_up: bfloat16 [4, 4, 256, 512], P('pipe'), may hold values from -0.375 to 0.375
- w_down: bfloat16 [4, 4, 4, 128, 256], P('pipe'), may hold values from -0.25 to 0.25
Outputs:
- first_tick: bfloat16 [4, 65536, 1024], P('pipe', 'seq')
- second_tick: bfloat16 [4, 65536, 1024], P('pipe', 'seq')
The draws below stay inside these ranges and needn't reach their ends.
All inputs are finite; a program needn't handle non-finite values.
Results may differ from the reference program's by a relative error of at most 0.007.
Values may be sent and summed in bfloat16 or wider, within the bound.
No kernel may reach another device: no remote copies, remote signals or barrier semaphores. Data moves between devices by JAX's collectives and lax.ppermute only.
A program may use at most 128 MiB of HBM per device.

```python
import jax
import jax.numpy as jnp
from jax import lax

D = 1024
NB = 4
BLOCK = 256
M = 256
SEQ = 65536
LAYERS = 4
DB = 256
FB = 512
Q = 128


def block_levels(key, extent, shards, smallest, high):
    loudness, own = 1.0, jax.random.fold_in(key, 6)
    for dim, shards_of in shards:
        draws = jnp.exp(jax.random.uniform(jax.random.fold_in(own, dim), (shards_of,), jnp.float32, smallest / len(shards), high / len(shards)))
        loudness = loudness * jnp.repeat(draws, extent[dim] // shards_of).reshape([-1 if axis == dim else 1 for axis in range(len(extent))])
    return loudness


def scatter_about(stream_key, extent, spread, bound, shards=(), kind=jnp.bfloat16):
    values = spread * jax.random.normal(stream_key, extent, jnp.float32)
    if shards:
        values = values * block_levels(stream_key, extent, shards, -0.22, 0.18)
    return jnp.clip(values, -bound, bound).astype(kind)


def setup_inputs(seed: int = 0) -> dict:
    key_of = jax.random.split(jax.random.key(seed), 10)
    in_flight = scatter_about(key_of[0], (LAYERS, SEQ, D), 1.0, 6.0, ((0, 4), (1, 64)))
    fresh_rows = scatter_about(key_of[1], (SEQ, D), 1.0, 6.0, ((0, 64),))
    right_factor = scatter_about(key_of[2], (LAYERS, M, BLOCK, BLOCK), BLOCK ** -0.5, 0.375, ((0, 4), (1, 64)))
    left_factor = scatter_about(key_of[3], (LAYERS, BLOCK, M, M), M ** -0.5, 0.375, ((0, 4), (1, 64)))
    gate_gain = scatter_about(key_of[4], (LAYERS, D), 1.0, 4.0, ((0, 4),), jnp.float32)
    gate_bias = scatter_about(key_of[5], (LAYERS, D), 1.0, 4.0, ((0, 4),), jnp.float32)
    norm_gain = jnp.clip(0.5 + 1.0 * jax.random.uniform(key_of[6], (LAYERS, D), jnp.float32) ** block_levels(key_of[6], (LAYERS, D), ((0, 4),), -0.2, 0.2), 0.5, 1.5)
    w_up = scatter_about(key_of[7], (LAYERS, NB, DB, FB), DB ** -0.5, 0.375, ((0, 4),))
    w_down = scatter_about(key_of[8], (LAYERS, NB, NB, Q, DB), FB ** -0.5, 0.25, ((0, 4),))
    return dict(in_flight=in_flight, fresh_rows=fresh_rows, right_factor=right_factor, left_factor=left_factor, gate_gain=gate_gain, gate_bias=gate_bias, norm_gain=norm_gain, w_up=w_up, w_down=w_down)


def one_layer(rows, right_blocks, left_blocks, gate_slope, gate_shift, gain, up_weight, down_weight):
    blocked = rows.reshape(M, BLOCK, D).astype(jnp.float32)
    first_mix = jnp.einsum('ikj,ijc->ikc', right_blocks.astype(jnp.float32), blocked).astype(jnp.bfloat16)
    second_mix = jnp.einsum('jpi,ijc->pjc', left_blocks.astype(jnp.float32), first_mix.astype(jnp.float32)).astype(jnp.bfloat16)
    mixed_seq = second_mix.reshape(M * BLOCK, D).astype(jnp.float32)
    input_wide = rows.astype(jnp.float32)
    residual = input_wide + mixed_seq * jax.nn.sigmoid(input_wide * gate_slope + gate_shift)
    scale_row = lax.rsqrt(lax.optimization_barrier(jnp.mean(residual * residual, axis=-1, keepdims=True)) + 1e-06)
    normed = (residual * scale_row * gain).astype(jnp.bfloat16)
    up_proj = jnp.einsum('tbd,bdf->tbf', normed.reshape(-1, NB, DB).astype(jnp.float32), up_weight.astype(jnp.float32))
    hidden = jax.nn.gelu(up_proj, approximate=True).astype(jnp.bfloat16)
    down_proj = jnp.einsum('tbkq,kbqe->tke', hidden.reshape(-1, NB, NB, Q).astype(jnp.float32), down_weight.astype(jnp.float32))
    return (residual + down_proj.reshape(-1, D)).astype(jnp.bfloat16)

def apply_layer(layer, rows, right_factor, left_factor, gate_gain, gate_bias, norm_gain, w_up, w_down):
    return one_layer(rows, right_factor[layer], left_factor[layer], gate_gain[layer], gate_bias[layer], norm_gain[layer], w_up[layer], w_down[layer])

def reference(in_flight, fresh_rows, right_factor, left_factor, gate_gain, gate_bias, norm_gain, w_up, w_down):
    first_list = []
    for layer in range(LAYERS):
        first_list.append(apply_layer(layer, in_flight[layer], right_factor, left_factor, gate_gain, gate_bias, norm_gain, w_up, w_down))
    second_list = []
    for layer in range(LAYERS):
        source = fresh_rows if layer == 0 else first_list[layer - 1]
        second_list.append(apply_layer(layer, source, right_factor, left_factor, gate_gain, gate_bias, norm_gain, w_up, w_down))
    return (jnp.stack(first_list, axis=0), jnp.stack(second_list, axis=0))
```

```python
import jax
import jax.numpy as jnp
from jax import lax
from jax.experimental import pallas as pl
from jax.experimental.pallas import tpu as pltpu
from jax.sharding import PartitionSpec as P


BLOCK = 256
WIDTH = 1024
DEVICES = 64
F32 = jnp.float32
BF16 = jnp.bfloat16
WHOLE = pl.BlockSpec(memory_space=pltpu.MemorySpace.VMEM)


def params(name):
    return dict(
        name=name,
        compiler_params=pltpu.CompilerParams(vmem_limit_bytes=48 * 1024 * 1024),
    )


def low_half(shape):
    return lax.broadcasted_iota(jnp.int32, shape, 1) < 4


def mix_first_tiles(right_ref, load_rows, blocks):
    tiles = []
    for pair in range(blocks // 2):
        even, odd = (
            jnp.dot(right_ref[block], load_rows(block), preferred_element_type=F32).reshape(
                BLOCK // 8, 8, -1
            )
            for block in (2 * pair, 2 * pair + 1)
        )
        low = low_half(even.shape)
        tiles.append(
            (
                jnp.where(low, even, pltpu.roll(odd, 4, 1)),
                jnp.where(low, pltpu.roll(even, 4, 1), odd),
            )
        )
    ordered = [tiles[pair][parity] for parity in range(2) for pair in range(blocks // 2)]
    return jnp.stack(ordered, axis=1).reshape(blocks * BLOCK, -1)


def first_kernel(right_ref, rows_ref, out_ref):
    blocks = right_ref.shape[0]
    load = lambda block: rows_ref[pl.ds(block * BLOCK, BLOCK), :]
    out_ref[...] = mix_first_tiles(right_ref, load, blocks).astype(BF16)


def mix_first(right, rows, chunk=256):
    blocks = right.shape[0]
    column = pl.BlockSpec((blocks * BLOCK, chunk), lambda c: (0, c))
    return pl.pallas_call(
        first_kernel,
        grid=(WIDTH // chunk,),
        in_specs=[pl.BlockSpec((blocks, BLOCK, BLOCK), lambda c: (0, 0, 0)), column],
        out_specs=column,
        out_shape=jax.ShapeDtypeStruct((blocks * BLOCK, WIDTH), BF16),
        **params("mix_first"),
    )(right, rows)


def select_first_kernel(segment_ref, right_ref, fresh_ref, received_ref, out_ref, current_ref):
    blocks = right_ref.shape[0]

    @pl.when(segment_ref[0] == 0)
    def _():
        current_ref[...] = fresh_ref[...]

    @pl.when(segment_ref[0] != 0)
    def _():
        current_ref[...] = received_ref[...]

    load = lambda block: current_ref[pl.ds(block * BLOCK, BLOCK), :]
    out_ref[...] = mix_first_tiles(right_ref, load, blocks).astype(BF16)


def select_mix_first(segment, right, fresh, received, half, chunk=512):
    rows = 2 * BLOCK
    column = pl.BlockSpec((rows, chunk), lambda c: (0, c))
    return pl.pallas_call(
        select_first_kernel,
        grid=(WIDTH // chunk,),
        in_specs=[
            pl.BlockSpec(memory_space=pltpu.MemorySpace.SMEM),
            pl.BlockSpec((2, BLOCK, BLOCK), lambda c: (half, 0, 0)),
            pl.BlockSpec((rows, chunk), lambda c: (half, c)),
            column,
        ],
        out_specs=(column, column),
        out_shape=(jax.ShapeDtypeStruct((rows, WIDTH), BF16),) * 2,
        **params("select_mix_first"),
    )(segment, right, fresh, received)


def spread(left, rows_order, columns_of):
    size = left.shape[-1]
    rows = rows_order(left).reshape(-1, size)
    source = jnp.repeat(columns_of, 4)
    place = (lax.broadcasted_iota(jnp.int32, (size, 4 * size), 0) == source[None]).astype(BF16)
    full = jnp.dot(rows, place, preferred_element_type=F32)
    row = lax.broadcasted_iota(jnp.int32, full.shape, 0)
    column = lax.broadcasted_iota(jnp.int32, full.shape, 1)
    return jnp.where(row % 4 == column % 4, full, 0.0).astype(BF16)


def spread_by_output_half(left):
    split = lambda a: a.reshape(4, DEVICES, 2, 2, BLOCK).transpose(2, 1, 3, 0, 4)
    return spread(left, split, jnp.arange(BLOCK))


def spread_by_input_half(left):
    order = jnp.arange(BLOCK).reshape(DEVICES, 2, 2).transpose(1, 0, 2).reshape(-1)
    return spread(left, lambda a: a.transpose(1, 0, 2), order)


def second_kernel(left_ref, *refs):
    *parts, out_ref = refs
    depth = left_ref.shape[1] // len(parts)
    total = sum(
        jnp.dot(
            left_ref[:, pl.ds(n * depth, depth)], part[...], preferred_element_type=F32
        )
        for n, part in enumerate(parts)
    )
    out_ref[...] = total.astype(BF16)


def mix_second(left, parts, half, rows, chunk=256):
    return pl.pallas_call(
        second_kernel,
        grid=(WIDTH // chunk,),
        in_specs=[pl.BlockSpec((rows, left.shape[1]), lambda c: (half, 0))]
        + [pl.BlockSpec((part.shape[0], chunk), lambda c: (0, c)) for part in parts],
        out_specs=pl.BlockSpec((rows, chunk), lambda c: (0, c)),
        out_shape=jax.ShapeDtypeStruct((rows, WIDTH), BF16),
        **params("mix_second"),
    )(left, *parts)


def channel_kernel(
    returned_ref, rows_ref, slope_ref, shift_ref, gain_ref, up_ref, down_ref, out_ref
):
    blocks, count, width = rows_ref.shape
    arrived = returned_ref[...].astype(F32).reshape(count // 8, 2, blocks // 2, 8, width)
    mixed = []
    for pair in range(blocks // 2):
        even, odd = arrived[:, 0, pair], arrived[:, 1, pair]
        low = low_half(even.shape)
        mixed.append(jnp.where(low, even, pltpu.roll(odd, 4, 1)).reshape(count, width))
        mixed.append(jnp.where(low, pltpu.roll(even, 4, 1), odd).reshape(count, width))
    for block in range(blocks):
        wide = rows_ref[block].astype(F32)
        gate = 0.5 * jnp.tanh(0.5 * (wide * slope_ref[...] + shift_ref[...])) + 0.5
        residual = wide + mixed[block] * gate
        scale = lax.rsqrt(jnp.mean(residual * residual, axis=-1, keepdims=True) + 1e-06)
        normed = (residual * scale * gain_ref[...]).astype(BF16)
        hidden = []
        for b in range(4):
            up = jnp.dot(normed[:, b * 256 : (b + 1) * 256], up_ref[b], preferred_element_type=F32)
            hidden.append(jax.nn.gelu(up, approximate=True).astype(BF16))
        for k in range(4):
            taken = jnp.concatenate([h[:, k * 128 : (k + 1) * 128] for h in hidden], axis=1)
            down = jnp.dot(taken, down_ref[k], preferred_element_type=F32)
            columns = slice(k * 256, (k + 1) * 256)
            out_ref[block, :, columns] = (residual[:, columns] + down).astype(BF16)


def channel_part(returned, rows, start, channel_weights, count=64):
    blocks = returned.shape[0] // BLOCK
    slope, shift, gain, up, down = channel_weights
    fixed = lambda a: pl.BlockSpec(a.shape, lambda s: (0,) * a.ndim)
    return pl.pallas_call(
        channel_kernel,
        grid=(BLOCK // count,),
        in_specs=[
            pl.BlockSpec((blocks * count, WIDTH), lambda s: (s, 0)),
            pl.BlockSpec((blocks, count, WIDTH), lambda s: (start, s, 0)),
            fixed(slope),
            fixed(shift),
            fixed(gain),
            fixed(up),
            fixed(down),
        ],
        out_specs=pl.BlockSpec((blocks, count, WIDTH), lambda s: (0, s, 0)),
        out_shape=jax.ShapeDtypeStruct((blocks, BLOCK, WIDTH), BF16),
        **params("channel_part"),
    )(returned, rows, *channel_weights).reshape(blocks * BLOCK, WIDTH)


def exchange(rows):
    grouped = rows.reshape(DEVICES, -1, WIDTH)
    return lax.all_to_all(grouped, "seq", split_axis=0, concat_axis=0, tiled=True).reshape(
        rows.shape
    )


def shards(
    in_flight, fresh_rows, right_factor, left_factor, gate_gain, gate_bias, norm_gain, w_up, w_down
):
    segment = lax.axis_index("pipe").reshape(1)
    rows, right, left = in_flight[0], right_factor[0], left_factor[0]
    weights = (gate_gain, gate_bias, norm_gain, w_up[0], w_down[0].reshape(4, 512, 256))
    route = [(n, n + 1) for n in range(lax.axis_size("pipe") - 1)]
    leaving = mix_first(right, rows)
    arrived = exchange(leaving)
    left_held, _ = lax.optimization_barrier((left, leaving))
    left_out = spread_by_output_half(left_held)
    left_in = spread_by_input_half(left_held)
    returned = []
    for half in range(2):
        mixed = mix_second(left_out, (arrived,), half, 512)
        returned.append(exchange(mixed))
    blocked = rows.reshape(4, BLOCK, WIDTH)
    firsts, currents, arrivals = [], [], []
    for half in range(2):
        out = channel_part(returned[half], blocked, half, weights)
        firsts.append(out)
        received = lax.ppermute(out, "pipe", route)
        leaving, current = select_mix_first(segment, right, fresh_rows, received, half)
        currents.append(current)
        arrivals.append(exchange(leaving))
    first_out = jnp.concatenate(firsts)
    current = jnp.concatenate(currents)
    mixed = mix_second(left_in, tuple(arrivals), 0, 1024)
    last = exchange(mixed)
    second_out = channel_part(last, current.reshape(4, BLOCK, WIDTH), 0, weights)
    return first_out[None], second_out[None]


def solution(mesh):
    in_specs = (
        P("pipe", "seq", None),
        P("seq", None),
        P("pipe", "seq", None, None),
        P("pipe", "seq", None, None),
        P("pipe", None),
        P("pipe", None),
        P("pipe", None),
        P("pipe", None, None, None),
        P("pipe", None, None, None, None),
    )
    out_specs = (P("pipe", "seq", None), P("pipe", "seq", None))
    return jax.shard_map(shards, mesh=mesh, in_specs=in_specs, out_specs=out_specs, check_vma=False)
```

```python
import functools

import jax
import jax.numpy as jnp
from jax import lax
from jax.experimental import pallas as pl
from jax.experimental.pallas import tpu as pltpu
from jax.sharding import PartitionSpec as P


BLOCK = 256
WIDTH = 1024
DEVICES = 64
F32 = jnp.float32
BF16 = jnp.bfloat16
HBM = pltpu.MemorySpace.HBM
VMEM = pltpu.MemorySpace.VMEM


def in_hbm(array):
    return pltpu.with_memory_space_constraint(array, HBM)


def in_vmem(array):
    return pltpu.with_memory_space_constraint(array, VMEM)


def params(name):
    return dict(
        name=name,
        compiler_params=pltpu.CompilerParams(vmem_limit_bytes=48 * 1024 * 1024),
    )


def low_half(shape):
    return lax.broadcasted_iota(jnp.int32, shape, 1) < 4


def mix_first_tiles(right_ref, load_rows, blocks):
    tiles = []
    for pair in range(blocks // 2):
        even, odd = (
            jnp.dot(right_ref[block], load_rows(block), preferred_element_type=F32).reshape(
                BLOCK // 8, 8, -1
            )
            for block in (2 * pair, 2 * pair + 1)
        )
        low = low_half(even.shape)
        tiles.append(
            (
                jnp.where(low, even, pltpu.roll(odd, 4, 1)),
                jnp.where(low, pltpu.roll(even, 4, 1), odd),
            )
        )
    ordered = [tiles[pair][parity] for parity in range(2) for pair in range(blocks // 2)]
    return jnp.stack(ordered, axis=1).reshape(blocks * BLOCK, -1)


def first_kernel(right_ref, *refs):
    *rows_refs, out_ref = refs
    blocks = right_ref.shape[0]

    def load(block):
        if len(rows_refs) > 1:
            return rows_refs[block][...]
        return rows_refs[0][pl.ds(block * BLOCK, BLOCK), :]

    out_ref[...] = mix_first_tiles(right_ref, load, blocks).astype(BF16)


def mix_first(right, parts, blocks, start, chunk):
    column = lambda rows: pl.BlockSpec((rows, chunk), lambda c: (0, c))
    return pl.pallas_call(
        first_kernel,
        grid=(WIDTH // chunk,),
        in_specs=[pl.BlockSpec((blocks, BLOCK, BLOCK), lambda c: (start, 0, 0))]
        + [column(part.shape[0]) for part in parts],
        out_specs=column(blocks * BLOCK),
        out_shape=HBM((blocks * BLOCK, WIDTH), BF16),
        **params("mix_first"),
    )(in_hbm(right), *parts)


def spread_kernel(half, rows_ref, out_ref):
    size = rows_ref.shape[1]
    chunk = 2 * size
    for start in range(0, out_ref.shape[1], chunk):
        column = start + lax.broadcasted_iota(jnp.int32, (size, chunk), 1)
        if half is None:
            source = column >> 2
        else:
            source = ((column >> 3) << 2) + 2 * half + ((column >> 2) & 1)
        place = jnp.where(lax.broadcasted_iota(jnp.int32, (size, chunk), 0) == source, 1.0, 0.0)
        full = jnp.dot(rows_ref[...], place.astype(BF16), preferred_element_type=F32)
        row = lax.broadcasted_iota(jnp.int32, full.shape, 0)
        offset = lax.broadcasted_iota(jnp.int32, full.shape, 1)
        kept = jnp.where((row & 3) == (offset & 3), full, 0.0)
        out_ref[:, start : start + chunk] = kept.astype(BF16)


def spread(rows, half=None):
    columns = 4 * BLOCK if half is None else 2 * BLOCK
    return pl.pallas_call(
        functools.partial(spread_kernel, half),
        out_shape=VMEM((4 * BLOCK, columns), BF16),
        **params("spread"),
    )(rows)


def rows_by_output_half(left):
    split = left.reshape(4, DEVICES, 2, 2, BLOCK).transpose(2, 1, 3, 0, 4)
    return split.reshape(-1, BLOCK)


def rows_by_output(left):
    return left.transpose(1, 0, 2).reshape(-1, BLOCK)


def second_kernel(start, left_ref, part_ref, *refs):
    *held_refs, out_ref = refs
    left = left_ref[pl.ds(start, out_ref.shape[0]), :]
    total = jnp.dot(left, part_ref[...], preferred_element_type=F32)
    for held_ref in held_refs:
        total = total + held_ref[...]
    out_ref[...] = total.astype(out_ref.dtype)


def mix_second(left, part, start, out_shape, held=(), chunk=256):
    column = lambda rows: pl.BlockSpec((rows, chunk), lambda c: (0, c))
    return pl.pallas_call(
        functools.partial(second_kernel, start),
        grid=(WIDTH // chunk,),
        in_specs=[pl.BlockSpec(memory_space=VMEM), column(part.shape[0])]
        + [column(array.shape[0]) for array in held],
        out_specs=column(out_shape.shape[0]),
        out_shape=out_shape,
        **params("mix_second"),
    )(in_vmem(left), in_vmem(part), *(in_hbm(array) for array in held))


def gelu(u):
    inner = u * (0.7978845608028654 + 0.035677408136300125 * (u * u))
    half = 0.5 * u
    return half + half * jnp.tanh(inner)


def channel_rows(which, arrived, rows_refs, weight_refs):
    slope_ref, shift_ref, gain_ref, up_ref, down_ref = weight_refs
    width = arrived.shape[-1]
    mixed = []
    for place in which:
        even, odd = arrived[:, 0, place // 2], arrived[:, 1, place // 2]
        low = low_half(even.shape)
        if place % 2:
            mixed.append(jnp.where(low, pltpu.roll(even, 4, 1), odd).reshape(-1, width))
        else:
            mixed.append(jnp.where(low, even, pltpu.roll(odd, 4, 1)).reshape(-1, width))
    mixed = jnp.concatenate(mixed)
    wide = jnp.concatenate([ref[...].reshape(-1, width) for ref in rows_refs]).astype(F32)
    gate = 0.5 * jnp.tanh(wide * (0.5 * slope_ref[...]) + 0.5 * shift_ref[...]) + 0.5
    residual = wide + mixed * gate
    scale = lax.rsqrt(jnp.mean(residual * residual, axis=-1, keepdims=True) + 1e-06)
    normed = (residual * scale * gain_ref[...]).astype(BF16)
    hidden = []
    for b in range(4):
        up = jnp.dot(normed[:, b * 256 : (b + 1) * 256], up_ref[b], preferred_element_type=F32)
        hidden.append(gelu(up).astype(BF16))
    out = []
    for k in range(4):
        taken = jnp.concatenate([h[:, k * 128 : (k + 1) * 128] for h in hidden], axis=1)
        down = jnp.dot(taken, down_ref[k], preferred_element_type=F32)
        out.append((residual[:, k * 256 : (k + 1) * 256] + down).astype(BF16))
    return jnp.concatenate(out, axis=1)


def arrived_tiles(returned_ref, pairs):
    width = returned_ref.shape[-1]
    return returned_ref[...].astype(F32).reshape(-1, 2, pairs, 8, width)


def relay_kernel(place, last_ref, returned_ref, rows_ref, fresh_ref, *refs):
    *weight_refs, out_ref, sent_ref = refs
    arrived = arrived_tiles(returned_ref, 1)
    out = channel_rows((place,), arrived, (rows_ref,), weight_refs)
    out_ref[...] = out

    @pl.when(last_ref[0] == 0)
    def _():
        sent_ref[...] = out

    @pl.when(last_ref[0] != 0)
    def _():
        sent_ref[...] = fresh_ref[...]


def fixed(array):
    return pl.BlockSpec(array.shape, lambda s: (0,) * array.ndim)


def channel_relay(last, returned, rows, fresh, block, weights, count=128):
    steps = BLOCK // count
    local = pl.BlockSpec((count, WIDTH), lambda s: (block * steps + s, 0))
    plain = pl.BlockSpec((count, WIDTH), lambda s: (s, 0))
    return pl.pallas_call(
        functools.partial(relay_kernel, block % 2),
        grid=(steps,),
        in_specs=[
            pl.BlockSpec(memory_space=pltpu.MemorySpace.SMEM),
            pl.BlockSpec((2 * count, WIDTH), lambda s: (s, 0)),
            local,
            local,
            *(fixed(array) for array in weights),
        ],
        out_specs=(plain, plain),
        out_shape=(HBM((BLOCK, WIDTH), BF16),) * 2,
        **params("channel_relay"),
    )(last, in_hbm(returned), in_hbm(rows), in_hbm(fresh), *weights)


def last_kernel(returned_ref, *refs):
    *rest, out_ref = refs
    rows_refs, weight_refs = rest[:4], rest[4:]
    arrived = arrived_tiles(returned_ref, 2)
    out = channel_rows((0, 1, 2, 3), arrived, rows_refs, weight_refs)
    out_ref[...] = out.reshape(out_ref.shape)


def channel_last(returned, parts, weights, count=64):
    plain = pl.BlockSpec((count, WIDTH), lambda s: (s, 0))
    return pl.pallas_call(
        last_kernel,
        grid=(BLOCK // count,),
        in_specs=[
            pl.BlockSpec((4 * count, WIDTH), lambda s: (s, 0)),
            *(plain for _ in parts),
            *(fixed(array) for array in weights),
        ],
        out_specs=pl.BlockSpec((4, count, WIDTH), lambda s: (0, s, 0)),
        out_shape=HBM((4, BLOCK, WIDTH), BF16),
        **params("channel_last"),
    )(in_hbm(returned), *parts, *weights)


def exchange(rows):
    grouped = rows.reshape(DEVICES, -1, WIDTH)
    return lax.all_to_all(grouped, "seq", split_axis=0, concat_axis=0, tiled=True).reshape(
        rows.shape
    )


def shards(
    in_flight, fresh_rows, right_factor, left_factor, gate_gain, gate_bias, norm_gain, w_up, w_down
):
    sections = lax.axis_size("pipe")
    last = (lax.axis_index("pipe") == sections - 1).astype(jnp.int32).reshape(1)
    rows, right, left = in_flight[0], right_factor[0], left_factor[0]
    weights = (gate_gain, gate_bias, norm_gain, w_up[0], w_down[0].reshape(4, 512, 256))
    route = [(n, (n + 1) % sections) for n in range(sections)]
    leaving = mix_first(right, (in_hbm(rows),), 4, 0, 256)
    arrived = exchange(leaving)
    left_held, _ = lax.optimization_barrier((left, leaving))
    left_out = spread(rows_by_output_half(left_held))
    by_output = rows_by_output(left_held)
    returned = []
    for half in range(2):
        mixed = mix_second(left_out, arrived, 512 * half, HBM((512, WIDTH), BF16))
        returned.append(exchange(mixed))
    firsts, currents, arrivals = [], [], []
    for half in range(2):
        for block in (2 * half, 2 * half + 1):
            out, sent = channel_relay(last, returned[half], rows, fresh_rows, block, weights)
            firsts.append(out)
            currents.append(in_hbm(lax.ppermute(sent, "pipe", route)))
        leaving = mix_first(right, currents[2 * half :], 2, half, 512)
        arrivals.append(exchange(leaving))
    first_out = jnp.concatenate(firsts)
    left_in = [spread(by_output, half) for half in range(2)]
    partial = mix_second(left_in[0], arrivals[0], 0, HBM((1024, WIDTH), F32))
    mixed = mix_second(
        left_in[1], arrivals[1], 0, HBM((1024, WIDTH), BF16), (partial,)
    )
    final = exchange(mixed)
    second_out = channel_last(final, currents, weights)
    return first_out[None], second_out.reshape(1, 1024, WIDTH)


def solution(mesh):
    in_specs = (
        P("pipe", "seq", None),
        P("seq", None),
        P("pipe", "seq", None, None),
        P("pipe", "seq", None, None),
        P("pipe", None),
        P("pipe", None),
        P("pipe", None),
        P("pipe", None, None, None),
        P("pipe", None, None, None, None),
    )
    out_specs = (P("pipe", "seq", None), P("pipe", "seq", None))
    return jax.shard_map(
        shards, mesh=mesh, in_specs=in_specs, out_specs=out_specs, check_vma=False
    )
```

```python
import functools

import jax
import jax.numpy as jnp
from jax import lax
from jax.experimental import pallas as pl
from jax.experimental.pallas import tpu as pltpu
from jax.sharding import PartitionSpec as P


BLOCK = 256
WIDTH = 1024
DEVICES = 64
F32 = jnp.float32
BF16 = jnp.bfloat16
HBM = pltpu.MemorySpace.HBM
VMEM = pltpu.MemorySpace.VMEM


def in_hbm(array):
    return pltpu.with_memory_space_constraint(array, HBM)


def in_vmem(array):
    return pltpu.with_memory_space_constraint(array, VMEM)


def params(name):
    return dict(
        name=name,
        compiler_params=pltpu.CompilerParams(vmem_limit_bytes=48 * 1024 * 1024),
    )


def low_half(shape):
    return lax.broadcasted_iota(jnp.int32, shape, 1) < 4


def mix_first_tiles(right_ref, load_rows, blocks):
    tiles = []
    for pair in range(blocks // 2):
        even, odd = (
            jnp.dot(right_ref[block], load_rows(block), preferred_element_type=F32).reshape(
                BLOCK // 8, 8, -1
            )
            for block in (2 * pair, 2 * pair + 1)
        )
        low = low_half(even.shape)
        tiles.append(
            (
                jnp.where(low, even, pltpu.roll(odd, 4, 1)),
                jnp.where(low, pltpu.roll(even, 4, 1), odd),
            )
        )
    ordered = [tiles[pair][parity] for parity in range(2) for pair in range(blocks // 2)]
    return jnp.stack(ordered, axis=1).reshape(blocks * BLOCK, -1)


def first_kernel(right_ref, rows_ref, out_ref):
    load = lambda block: rows_ref[pl.ds(block * BLOCK, BLOCK), :]
    out_ref[...] = mix_first_tiles(right_ref, load, right_ref.shape[0]).astype(BF16)


def mix_first(right, rows, chunk=256):
    column = pl.BlockSpec((rows.shape[0], chunk), lambda c: (0, c))
    return pl.pallas_call(
        first_kernel,
        grid=(WIDTH // chunk,),
        in_specs=[pl.BlockSpec(right.shape, lambda c: (0, 0, 0)), column],
        out_specs=column,
        out_shape=HBM(rows.shape, BF16),
        **params("mix_first"),
    )(in_hbm(right), in_hbm(rows))


def relayed_kernel(half, chunk, section_ref, right_ref, fresh_ref, *refs):
    *received_refs, out_ref, current_ref, sem = refs
    columns = pl.ds(pl.program_id(0) * chunk, chunk)

    @pl.when(section_ref[0] == 0)
    def _():
        source = fresh_ref.at[pl.ds(2 * half * BLOCK, 2 * BLOCK), columns]
        copy = pltpu.make_async_copy(source, current_ref, sem)
        copy.start()
        copy.wait()

    @pl.when(section_ref[0] != 0)
    def _():
        for block, received_ref in enumerate(received_refs):
            current_ref[pl.ds(block * BLOCK, BLOCK), :] = received_ref[:, columns]

    load = lambda block: current_ref[pl.ds(block * BLOCK, BLOCK), :]
    out_ref[...] = mix_first_tiles(right_ref, load, 2).astype(BF16)


def mix_first_relayed(section, right, fresh, received, half, chunk=512):
    column = pl.BlockSpec((2 * BLOCK, chunk), lambda c: (0, c))
    return pl.pallas_call(
        functools.partial(relayed_kernel, half, chunk),
        grid=(WIDTH // chunk,),
        in_specs=[
            pl.BlockSpec(memory_space=pltpu.MemorySpace.SMEM),
            pl.BlockSpec((2, BLOCK, BLOCK), lambda c: (half, 0, 0)),
            pl.BlockSpec(memory_space=pl.ANY),
            *(pl.BlockSpec(memory_space=VMEM) for _ in received),
        ],
        out_specs=(column, column),
        out_shape=(HBM((2 * BLOCK, WIDTH), BF16),) * 2,
        scratch_shapes=[pltpu.SemaphoreType.DMA],
        **params("mix_first_relayed"),
    )(section, right, in_hbm(fresh), *(in_vmem(part) for part in received))


def spread_kernel(half, rows_ref, out_ref):
    size = rows_ref.shape[1]
    chunk = 2 * size
    for start in range(0, out_ref.shape[1], chunk):
        column = start + lax.broadcasted_iota(jnp.int32, (size, chunk), 1)
        if half is None:
            source = column >> 2
        else:
            source = ((column >> 3) << 2) + 2 * half + ((column >> 2) & 1)
        place = jnp.where(lax.broadcasted_iota(jnp.int32, (size, chunk), 0) == source, 1.0, 0.0)
        full = jnp.dot(rows_ref[...], place.astype(BF16), preferred_element_type=F32)
        row = lax.broadcasted_iota(jnp.int32, full.shape, 0)
        offset = lax.broadcasted_iota(jnp.int32, full.shape, 1)
        kept = jnp.where((row & 3) == (offset & 3), full, 0.0)
        out_ref[:, start : start + chunk] = kept.astype(BF16)


def spread(rows, half=None):
    columns = 4 * BLOCK if half is None else 2 * BLOCK
    return pl.pallas_call(
        functools.partial(spread_kernel, half),
        out_shape=VMEM((rows.shape[0], columns), BF16),
        **params("spread"),
    )(rows)


def rows_by_output_half(left):
    split = left.reshape(4, DEVICES, 2, 2, BLOCK).transpose(2, 1, 3, 0, 4)
    return split.reshape(-1, BLOCK)


def rows_by_output(left):
    return left.transpose(1, 0, 2).reshape(-1, BLOCK)


def second_kernel(left_ref, part_ref, *refs):
    *held_refs, out_ref = refs
    total = jnp.dot(left_ref[...], part_ref[...], preferred_element_type=F32)
    for held_ref in held_refs:
        total = total + held_ref[...]
    out_ref[...] = total.astype(out_ref.dtype)


def mix_second(left, part, out_shape, held=(), chunk=256):
    column = lambda rows: pl.BlockSpec((rows, chunk), lambda c: (0, c))
    return pl.pallas_call(
        second_kernel,
        grid=(WIDTH // chunk,),
        in_specs=[pl.BlockSpec(memory_space=VMEM), column(part.shape[0])]
        + [column(array.shape[0]) for array in held],
        out_specs=column(out_shape.shape[0]),
        out_shape=out_shape,
        **params("mix_second"),
    )(in_vmem(left), in_vmem(part), *(in_hbm(array) for array in held))


def gelu(u):
    inner = u * (0.7978845608028654 + 0.035677408136300125 * (u * u))
    half = 0.5 * u
    return half + half * jnp.tanh(inner)


def channel_rows(which, arrived, rows_refs, weight_refs):
    slope_ref, shift_ref, gain_ref, up_ref, down_ref = weight_refs
    width = arrived.shape[-1]
    mixed = []
    for place in which:
        even, odd = arrived[:, 0, place // 2], arrived[:, 1, place // 2]
        low = low_half(even.shape)
        if place % 2:
            mixed.append(jnp.where(low, pltpu.roll(even, 4, 1), odd).reshape(-1, width))
        else:
            mixed.append(jnp.where(low, even, pltpu.roll(odd, 4, 1)).reshape(-1, width))
    mixed = jnp.concatenate(mixed)
    wide = jnp.concatenate([ref[...].reshape(-1, width) for ref in rows_refs]).astype(F32)
    gate = 0.5 * jnp.tanh(wide * (0.5 * slope_ref[...]) + 0.5 * shift_ref[...]) + 0.5
    residual = wide + mixed * gate
    scale = lax.rsqrt(jnp.mean(residual * residual, axis=-1, keepdims=True) + 1e-06)
    normed = (residual * scale * gain_ref[...]).astype(BF16)
    hidden = []
    for b in range(4):
        up = jnp.dot(normed[:, b * 256 : (b + 1) * 256], up_ref[b], preferred_element_type=F32)
        hidden.append(gelu(up).astype(BF16))
    out = []
    for k in range(4):
        taken = jnp.concatenate([h[:, k * 128 : (k + 1) * 128] for h in hidden], axis=1)
        down = jnp.dot(taken, down_ref[k], preferred_element_type=F32)
        out.append((residual[:, k * 256 : (k + 1) * 256] + down).astype(BF16))
    return jnp.concatenate(out, axis=1)


def arrived_tiles(returned_ref, pairs):
    width = returned_ref.shape[-1]
    return returned_ref[...].astype(F32).reshape(-1, 2, pairs, 8, width)


def relay_kernel(place, returned_ref, rows_ref, *refs):
    *weight_refs, out_ref = refs
    arrived = arrived_tiles(returned_ref, 1)
    out_ref[...] = channel_rows((place,), arrived, (rows_ref,), weight_refs)


def fixed(array):
    return pl.BlockSpec(array.shape, lambda s: (0,) * array.ndim)


def channel_relay(returned, rows, block, weights, count=128):
    steps = BLOCK // count
    return pl.pallas_call(
        functools.partial(relay_kernel, block % 2),
        grid=(steps,),
        in_specs=[
            pl.BlockSpec((2 * count, WIDTH), lambda s: (s, 0)),
            pl.BlockSpec((count, WIDTH), lambda s: (block * steps + s, 0)),
            *(fixed(array) for array in weights),
        ],
        out_specs=pl.BlockSpec((count, WIDTH), lambda s: (s, 0)),
        out_shape=HBM((BLOCK, WIDTH), BF16),
        **params("channel_relay"),
    )(in_vmem(returned) if block % 2 == 0 else in_hbm(returned), in_hbm(rows), *weights)


def last_kernel(returned_ref, *refs):
    *rest, out_ref = refs
    rows_refs, weight_refs = rest[:2], rest[2:]
    arrived = arrived_tiles(returned_ref, 2)
    out = channel_rows((0, 1, 2, 3), arrived, rows_refs, weight_refs)
    out_ref[...] = out.reshape(out_ref.shape)


def channel_last(returned, parts, weights, count=64):
    pair = pl.BlockSpec((2, count, WIDTH), lambda s: (0, s, 0))
    return pl.pallas_call(
        last_kernel,
        grid=(BLOCK // count,),
        in_specs=[
            pl.BlockSpec((4 * count, WIDTH), lambda s: (s, 0)),
            *(pair for _ in parts),
            *(fixed(array) for array in weights),
        ],
        out_specs=pl.BlockSpec((4, count, WIDTH), lambda s: (0, s, 0)),
        out_shape=HBM((4, BLOCK, WIDTH), BF16),
        **params("channel_last"),
    )(in_hbm(returned), *(in_hbm(p) for p in parts), *weights)


def exchange(rows):
    grouped = rows.reshape(DEVICES, -1, WIDTH)
    return lax.all_to_all(grouped, "seq", split_axis=0, concat_axis=0, tiled=True).reshape(
        rows.shape
    )


def shards(
    in_flight, fresh_rows, right_factor, left_factor, gate_gain, gate_bias, norm_gain, w_up, w_down
):
    section = lax.axis_index("pipe").reshape(1)
    rows, right, left = in_flight[0], right_factor[0], left_factor[0]
    weights = (gate_gain, gate_bias, norm_gain, w_up[0], w_down[0].reshape(4, 512, 256))
    route = [(n, n + 1) for n in range(lax.axis_size("pipe") - 1)]
    leaving = mix_first(right, rows)
    arrived = exchange(leaving)
    left_held, _ = lax.optimization_barrier((left, leaving))
    left_out = rows_by_output_half(left_held)
    by_output = rows_by_output(left_held)
    returned = []
    for half in range(2):
        matrix = spread(left_out[512 * half : 512 * half + 512])
        mixed = mix_second(matrix, arrived, HBM((512, WIDTH), BF16))
        returned.append(exchange(mixed))
    firsts, currents, arrivals = [], [], []
    for half in range(2):
        received = []
        for block in (2 * half, 2 * half + 1):
            out = channel_relay(returned[half], rows, block, weights)
            firsts.append(out)
            received.append(lax.ppermute(out, "pipe", route))
        leaving, current = mix_first_relayed(section, right, fresh_rows, received, half)
        currents.append(current.reshape(2, BLOCK, WIDTH))
        arrivals.append(exchange(leaving))
    first_out = jnp.concatenate(firsts)
    left_in = [spread(by_output, half) for half in range(2)]
    partial = mix_second(left_in[0], arrivals[0], HBM((1024, WIDTH), F32))
    mixed = mix_second(left_in[1], arrivals[1], HBM((1024, WIDTH), BF16), (partial,))
    final = exchange(mixed)
    second_out = channel_last(final, currents, weights)
    return first_out[None], second_out.reshape(1, 1024, WIDTH)


def solution(mesh):
    in_specs = (
        P("pipe", "seq", None),
        P("seq", None),
        P("pipe", "seq", None, None),
        P("pipe", "seq", None, None),
        P("pipe", None),
        P("pipe", None),
        P("pipe", None),
        P("pipe", None, None, None),
        P("pipe", None, None, None, None),
    )
    out_specs = (P("pipe", "seq", None), P("pipe", "seq", None))
    return jax.shard_map(
        shards, mesh=mesh, in_specs=in_specs, out_specs=out_specs, check_vma=False
    )
```

```python
import functools

import jax
import jax.numpy as jnp
from jax import lax
from jax.experimental import pallas as pl
from jax.experimental.pallas import tpu as pltpu
from jax.sharding import PartitionSpec as P


BLOCK = 256
WIDTH = 1024
DEVICES = 64
F32 = jnp.float32
BF16 = jnp.bfloat16
HBM = pltpu.MemorySpace.HBM
VMEM = pltpu.MemorySpace.VMEM


def in_hbm(array):
    return pltpu.with_memory_space_constraint(array, HBM)


def in_vmem(array):
    return pltpu.with_memory_space_constraint(array, VMEM)


def params(name):
    return dict(
        name=name,
        compiler_params=pltpu.CompilerParams(vmem_limit_bytes=32 * 1024 * 1024),
    )


def low_half(shape):
    return lax.broadcasted_iota(jnp.int32, shape, 1) < 4


def mix_first_tiles(right_ref, load_rows, blocks):
    tiles = []
    for pair in range(blocks // 2):
        even, odd = (
            jnp.dot(right_ref[block], load_rows(block), preferred_element_type=F32).reshape(
                BLOCK // 8, 8, -1
            )
            for block in (2 * pair, 2 * pair + 1)
        )
        low = low_half(even.shape)
        tiles.append(
            (
                jnp.where(low, even, pltpu.roll(odd, 4, 1)),
                jnp.where(low, pltpu.roll(even, 4, 1), odd),
            )
        )
    ordered = [tiles[pair][parity] for parity in range(2) for pair in range(blocks // 2)]
    return jnp.stack(ordered, axis=1).reshape(blocks * BLOCK, -1)


def first_kernel(right_ref, rows_ref, out_ref):
    load = lambda block: rows_ref[pl.ds(block * BLOCK, BLOCK), :]
    out_ref[...] = mix_first_tiles(right_ref, load, right_ref.shape[0]).astype(BF16)


def mix_first(right, rows, chunk=256):
    column = pl.BlockSpec((rows.shape[0], chunk), lambda c: (0, c))
    return pl.pallas_call(
        first_kernel,
        grid=(WIDTH // chunk,),
        in_specs=[pl.BlockSpec(right.shape, lambda c: (0, 0, 0)), column],
        out_specs=column,
        out_shape=HBM(rows.shape, BF16),
        **params("mix_first"),
    )(in_hbm(right), in_hbm(rows))


def relayed_kernel(half, chunk, section_ref, right_ref, fresh_ref, *refs):
    *received_refs, out_ref, current_ref, held_ref, sems = refs
    step = pl.program_id(0)
    columns = pl.ds(step * chunk, chunk)

    def fetch(n):
        place = pl.ds(n * chunk, chunk)
        source = fresh_ref.at[pl.ds(2 * half * BLOCK, 2 * BLOCK), place]
        return pltpu.make_async_copy(source, held_ref.at[n], sems.at[n])

    @pl.when(section_ref[0] == 0)
    def _():
        @pl.when(step == 0)
        def _():
            for n in range(WIDTH // chunk):
                fetch(n).start()

        fetch(step).wait()
        current_ref[...] = held_ref[step]

    @pl.when(section_ref[0] != 0)
    def _():
        for block, received_ref in enumerate(received_refs):
            current_ref[pl.ds(block * BLOCK, BLOCK), :] = received_ref[:, columns]

    load = lambda block: current_ref[pl.ds(block * BLOCK, BLOCK), :]
    out_ref[...] = mix_first_tiles(right_ref, load, 2).astype(BF16)


def mix_first_relayed(section, right, fresh, received, half, chunk=512):
    column = pl.BlockSpec((2 * BLOCK, chunk), lambda c: (0, c))
    return pl.pallas_call(
        functools.partial(relayed_kernel, half, chunk),
        grid=(WIDTH // chunk,),
        in_specs=[
            pl.BlockSpec(memory_space=pltpu.MemorySpace.SMEM),
            pl.BlockSpec((2, BLOCK, BLOCK), lambda c: (half, 0, 0)),
            pl.BlockSpec(memory_space=pl.ANY),
            *(pl.BlockSpec(memory_space=VMEM) for _ in received),
        ],
        out_specs=(column, column),
        out_shape=(HBM((2 * BLOCK, WIDTH), BF16),) * 2,
        scratch_shapes=[
            VMEM((WIDTH // chunk, 2 * BLOCK, chunk), BF16),
            pltpu.SemaphoreType.DMA((WIDTH // chunk,)),
        ],
        **params("mix_first_relayed"),
    )(section, right, in_hbm(fresh), *(in_vmem(part) for part in received))


def spread_kernel(half, rows_ref, out_ref):
    size = rows_ref.shape[1]
    chunk = 2 * size
    for start in range(0, out_ref.shape[1], chunk):
        column = start + lax.broadcasted_iota(jnp.int32, (size, chunk), 1)
        if half is None:
            source = column >> 2
        else:
            source = ((column >> 3) << 2) + 2 * half + ((column >> 2) & 1)
        place = jnp.where(lax.broadcasted_iota(jnp.int32, (size, chunk), 0) == source, 0.5, 0.0)
        full = jnp.dot(rows_ref[...], place.astype(BF16), preferred_element_type=F32)
        row = lax.broadcasted_iota(jnp.int32, full.shape, 0)
        offset = lax.broadcasted_iota(jnp.int32, full.shape, 1)
        kept = jnp.where((row & 3) == (offset & 3), full, 0.0)
        out_ref[:, start : start + chunk] = kept.astype(BF16)


def spread(rows, half=None):
    columns, place = (4 * BLOCK, VMEM) if half is None else (2 * BLOCK, HBM)
    return pl.pallas_call(
        functools.partial(spread_kernel, half),
        out_shape=place((rows.shape[0], columns), BF16),
        **params("spread"),
    )(rows)


def rows_by_output_half(left):
    split = left.reshape(4, DEVICES, 2, 2, BLOCK).transpose(2, 1, 3, 0, 4)
    return split.reshape(-1, BLOCK)


def rows_by_output(left):
    return left.transpose(1, 0, 2).reshape(-1, BLOCK)


def second_kernel(*refs):
    *in_refs, out_ref = refs
    total = sum(
        jnp.dot(left_ref[...], part_ref[...], preferred_element_type=F32)
        for left_ref, part_ref in zip(in_refs[0::2], in_refs[1::2])
    )
    out_ref[...] = total.astype(BF16)


def mix_second_last(lefts, parts, count=256):
    rows = lefts[0].shape[0]
    block = lambda width: pl.BlockSpec((count, width), lambda r: (r, 0))
    specs, arrays = [], []
    for left, part in zip(lefts, parts):
        specs += [block(left.shape[1]), pl.BlockSpec(memory_space=VMEM)]
        arrays += [in_hbm(left), in_vmem(part)]
    return pl.pallas_call(
        second_kernel,
        grid=(rows // count,),
        in_specs=specs,
        out_specs=block(WIDTH),
        out_shape=HBM((rows, WIDTH), BF16),
        **params("mix_second_last"),
    )(*arrays)


def mix_second(pairs, chunk=256):
    rows = pairs[0][0].shape[0]
    column = lambda count: pl.BlockSpec((count, chunk), lambda c: (0, c))
    specs, arrays = [], []
    for left, part, place in pairs:
        specs += [pl.BlockSpec(memory_space=VMEM), column(part.shape[0])]
        arrays += [in_vmem(left), place(part)]
    return pl.pallas_call(
        second_kernel,
        grid=(WIDTH // chunk,),
        in_specs=specs,
        out_specs=column(rows),
        out_shape=HBM((rows, WIDTH), BF16),
        **params("mix_second"),
    )(*arrays)


def gelu_of_twice(v):
    inner = v * (v * v * BF16(8 * 0.7978845608028654 * 0.044715) + BF16(2 * 0.7978845608028654))
    return v + v * jnp.tanh(inner)


def channel_rows(which, arrived, rows_refs, weight_refs):
    slope_ref, shift_ref, gain_ref, up_ref, down_ref = weight_refs
    width = arrived.shape[-1]
    mixed = []
    for place in which:
        even, odd = arrived[:, 0, place // 2], arrived[:, 1, place // 2]
        low = low_half(even.shape)
        if place % 2:
            mixed.append(jnp.where(low, pltpu.roll(even, 4, 1), odd).reshape(-1, width))
        else:
            mixed.append(jnp.where(low, even, pltpu.roll(odd, 4, 1)).reshape(-1, width))
    mixed = jnp.concatenate(mixed)
    wide = jnp.concatenate([ref[...].reshape(-1, width) for ref in rows_refs]).astype(F32)
    gate = jnp.tanh(wide * (0.5 * slope_ref[...]) + 0.5 * shift_ref[...])
    residual = wide + mixed + mixed * gate
    scale = lax.rsqrt(jnp.mean(residual * residual, axis=-1, keepdims=True) + 1e-06)
    normed = (residual * scale * (0.5 * gain_ref[...])).astype(BF16)
    hidden = []
    for b in range(4):
        up = jnp.dot(normed[:, b * 256 : (b + 1) * 256], up_ref[b], preferred_element_type=F32)
        hidden.append(gelu_of_twice(up.astype(BF16)))
    out = []
    for k in range(4):
        taken = jnp.concatenate([h[:, k * 128 : (k + 1) * 128] for h in hidden], axis=1)
        down = jnp.dot(taken, down_ref[k], preferred_element_type=F32)
        out.append((residual[:, k * 256 : (k + 1) * 256] + down).astype(BF16))
    return jnp.concatenate(out, axis=1)


def arrived_tiles(returned_ref, pairs):
    width = returned_ref.shape[-1]
    return returned_ref[...].astype(F32).reshape(-1, 2, pairs, 8, width)


def relay_kernel(place, returned_ref, rows_ref, *refs):
    *weight_refs, out_ref = refs
    arrived = arrived_tiles(returned_ref, 1)
    out_ref[...] = channel_rows((place,), arrived, (rows_ref,), weight_refs)


def fixed(array):
    return pl.BlockSpec(array.shape, lambda s: (0,) * array.ndim)


def channel_relay(returned, rows, block, weights, count=128):
    first = block % 2 == 0
    steps = BLOCK // count
    start = 0 if first else block * steps
    if first:
        rows = in_vmem(rows[block * BLOCK : (block + 1) * BLOCK])
        returned = in_vmem(returned)
    else:
        rows, returned = in_hbm(rows), in_hbm(returned)
    return pl.pallas_call(
        functools.partial(relay_kernel, block % 2),
        grid=(steps,),
        in_specs=[
            pl.BlockSpec((2 * count, WIDTH), lambda s: (s, 0)),
            pl.BlockSpec((count, WIDTH), lambda s: (start + s, 0)),
            *(fixed(array) for array in weights),
        ],
        out_specs=pl.BlockSpec((count, WIDTH), lambda s: (s, 0)),
        out_shape=HBM((BLOCK, WIDTH), BF16),
        **params("channel_relay"),
    )(returned, rows, *weights)


def last_kernel(returned_ref, *refs):
    *rest, out_ref = refs
    rows_refs, weight_refs = rest[:2], rest[2:]
    arrived = arrived_tiles(returned_ref, 2)
    out = channel_rows((0, 1, 2, 3), arrived, rows_refs, weight_refs)
    out_ref[...] = out.reshape(out_ref.shape)


def channel_last(returned, parts, weights, count=64):
    pair = pl.BlockSpec((2, count, WIDTH), lambda s: (0, s, 0))
    return pl.pallas_call(
        last_kernel,
        grid=(BLOCK // count,),
        in_specs=[
            pl.BlockSpec((4 * count, WIDTH), lambda s: (s, 0)),
            *(pair for _ in parts),
            *(fixed(array) for array in weights),
        ],
        out_specs=pl.BlockSpec((4, count, WIDTH), lambda s: (0, s, 0)),
        out_shape=HBM((4, BLOCK, WIDTH), BF16),
        **params("channel_last"),
    )(in_hbm(returned), *(in_hbm(p) for p in parts), *weights)


def exchange(rows):
    grouped = rows.reshape(DEVICES, -1, WIDTH)
    return lax.all_to_all(grouped, "seq", split_axis=0, concat_axis=0, tiled=True).reshape(
        rows.shape
    )


def shards(
    in_flight, fresh_rows, right_factor, left_factor, gate_gain, gate_bias, norm_gain, w_up, w_down
):
    section = lax.axis_index("pipe").reshape(1)
    rows, right, left = in_flight[0], right_factor[0], left_factor[0]
    weights = (gate_gain, gate_bias, norm_gain, w_up[0], w_down[0].reshape(4, 512, 256))
    route = [(n, n + 1) for n in range(lax.axis_size("pipe") - 1)]
    leaving = mix_first(right, rows)
    arrived = exchange(leaving)
    left_held, _ = lax.optimization_barrier((left, leaving))
    left_out = rows_by_output_half(left_held)
    by_output = rows_by_output(left_held)
    returned = []
    for half in range(2):
        matrix = spread(left_out[512 * half : 512 * half + 512])
        mixed = mix_second([(matrix, arrived, in_vmem)])
        returned.append(exchange(mixed))
    firsts, currents, arrivals = [], [], []
    for half in range(2):
        received = []
        for block in (2 * half, 2 * half + 1):
            out = channel_relay(returned[half], rows, block, weights)
            firsts.append(out)
            received.append(lax.ppermute(out, "pipe", route))
        leaving, current = mix_first_relayed(section, right, fresh_rows, received, half)
        currents.append(current.reshape(2, BLOCK, WIDTH))
        arrivals.append(exchange(leaving))
    first_out = jnp.concatenate(firsts)
    mixed = mix_second_last([spread(by_output, half) for half in range(2)], arrivals)
    final = exchange(mixed)
    second_out = channel_last(final, currents, weights)
    return first_out[None], second_out.reshape(1, 1024, WIDTH)


def solution(mesh):
    in_specs = (
        P("pipe", "seq", None),
        P("seq", None),
        P("pipe", "seq", None, None),
        P("pipe", "seq", None, None),
        P("pipe", None),
        P("pipe", None),
        P("pipe", None),
        P("pipe", None, None, None),
        P("pipe", None, None, None, None),
    )
    out_specs = (P("pipe", "seq", None), P("pipe", "seq", None))
    return jax.shard_map(
        shards, mesh=mesh, in_specs=in_specs, out_specs=out_specs, check_vma=False
    )
```

```python
import functools

import jax
import jax.numpy as jnp
from jax import lax
from jax.experimental import pallas as pl
from jax.experimental.pallas import tpu as pltpu
from jax.sharding import PartitionSpec as P


BLOCK = 256
WIDTH = 1024
DEVICES = 64
F32 = jnp.float32
BF16 = jnp.bfloat16
HBM = pltpu.MemorySpace.HBM
VMEM = pltpu.MemorySpace.VMEM


def in_hbm(array):
    return pltpu.with_memory_space_constraint(array, HBM)


def in_vmem(array):
    return pltpu.with_memory_space_constraint(array, VMEM)


def params(name):
    return dict(
        name=name,
        compiler_params=pltpu.CompilerParams(vmem_limit_bytes=32 * 1024 * 1024),
    )


def low_half(shape):
    return lax.broadcasted_iota(jnp.int32, shape, 1) < 4


def mix_first_tiles(right_ref, load_rows, blocks):
    tiles = []
    for pair in range(blocks // 2):
        even, odd = (
            jnp.dot(right_ref[block], load_rows(block), preferred_element_type=F32).reshape(
                BLOCK // 8, 8, -1
            )
            for block in (2 * pair, 2 * pair + 1)
        )
        low = low_half(even.shape)
        tiles.append(
            (
                jnp.where(low, even, pltpu.roll(odd, 4, 1)),
                jnp.where(low, pltpu.roll(even, 4, 1), odd),
            )
        )
    ordered = [tiles[pair][parity] for parity in range(2) for pair in range(blocks // 2)]
    return jnp.stack(ordered, axis=1).reshape(blocks * BLOCK, -1)


def first_kernel(right_ref, rows_ref, out_ref):
    load = lambda block: rows_ref[pl.ds(block * BLOCK, BLOCK), :]
    tiles = mix_first_tiles(right_ref, load, 2).astype(BF16)
    out_ref[...] = tiles.reshape(out_ref.shape)


def mix_first(right, rows, chunk=512):
    count = rows.shape[0]
    out = pl.pallas_call(
        first_kernel,
        grid=(count // (2 * BLOCK), WIDTH // chunk),
        in_specs=[
            pl.BlockSpec((2, BLOCK, BLOCK), lambda h, c: (h, 0, 0)),
            pl.BlockSpec((2 * BLOCK, chunk), lambda h, c: (h, c)),
        ],
        out_specs=pl.BlockSpec((DEVICES, 1, 8, chunk), lambda h, c: (0, h, 0, c)),
        out_shape=HBM((DEVICES, count // (2 * BLOCK), 8, WIDTH), BF16),
        **params("mix_first"),
    )(in_hbm(right), in_hbm(rows))
    return out.reshape(count, WIDTH)


def relayed_kernel(half, chunk, section_ref, right_ref, fresh_ref, *refs):
    *received_refs, out_ref, current_ref, held_ref, sems = refs
    step = pl.program_id(0)
    columns = pl.ds(step * chunk, chunk)

    def fetch(n):
        place = pl.ds(n * chunk, chunk)
        source = fresh_ref.at[pl.ds(2 * half * BLOCK, 2 * BLOCK), place]
        return pltpu.make_async_copy(source, held_ref.at[n], sems.at[n])

    @pl.when(section_ref[0] == 0)
    def _():
        @pl.when(step == 0)
        def _():
            for n in range(WIDTH // chunk):
                fetch(n).start()

        fetch(step).wait()
        current_ref[...] = held_ref[step]

    @pl.when(section_ref[0] != 0)
    def _():
        for block, received_ref in enumerate(received_refs):
            current_ref[pl.ds(block * BLOCK, BLOCK), :] = received_ref[:, columns]

    load = lambda block: current_ref[pl.ds(block * BLOCK, BLOCK), :]
    out_ref[...] = mix_first_tiles(right_ref, load, 2).astype(BF16)


def mix_first_relayed(section, right, fresh, received, half, chunk=512):
    column = pl.BlockSpec((2 * BLOCK, chunk), lambda c: (0, c))
    return pl.pallas_call(
        functools.partial(relayed_kernel, half, chunk),
        grid=(WIDTH // chunk,),
        in_specs=[
            pl.BlockSpec(memory_space=pltpu.MemorySpace.SMEM),
            pl.BlockSpec((2, BLOCK, BLOCK), lambda c: (half, 0, 0)),
            pl.BlockSpec(memory_space=pl.ANY),
            *(pl.BlockSpec(memory_space=VMEM) for _ in received),
        ],
        out_specs=(column, column),
        out_shape=(HBM((2 * BLOCK, WIDTH), BF16),) * 2,
        scratch_shapes=[
            VMEM((WIDTH // chunk, 2 * BLOCK, chunk), BF16),
            pltpu.SemaphoreType.DMA((WIDTH // chunk,)),
        ],
        **params("mix_first_relayed"),
    )(section, in_hbm(right), in_hbm(fresh), *(in_vmem(part) for part in received))


def spread_kernel(half, rows_ref, out_ref):
    size = rows_ref.shape[1]
    chunk = 2 * size
    for start in range(0, out_ref.shape[1], chunk):
        column = start + lax.broadcasted_iota(jnp.int32, (size, chunk), 1)
        if half is None:
            source = column >> 2
        else:
            source = ((column >> 3) << 2) + 2 * half + ((column >> 2) & 1)
        place = jnp.where(lax.broadcasted_iota(jnp.int32, (size, chunk), 0) == source, 0.5, 0.0)
        full = jnp.dot(rows_ref[...], place.astype(BF16), preferred_element_type=F32)
        row = lax.broadcasted_iota(jnp.int32, full.shape, 0)
        offset = lax.broadcasted_iota(jnp.int32, full.shape, 1)
        kept = jnp.where((row & 3) == (offset & 3), full, 0.0)
        out_ref[:, start : start + chunk] = kept.astype(BF16)


def spread(rows, half=None):
    columns = 4 * BLOCK if half is None else 2 * BLOCK
    return pl.pallas_call(
        functools.partial(spread_kernel, half),
        out_shape=VMEM((rows.shape[0], columns), BF16),
        **params("spread"),
    )(rows)


def rows_by_output_half(left):
    split = left.reshape(4, DEVICES, 2, 2, BLOCK).transpose(2, 1, 3, 0, 4)
    return split.reshape(-1, BLOCK)


def rows_by_output(left):
    return left.transpose(1, 0, 2).reshape(-1, BLOCK)


def second_kernel(left_ref, part_ref, *refs):
    *held_refs, out_ref = refs
    total = jnp.dot(left_ref[...], part_ref[...], preferred_element_type=F32)
    for held_ref in held_refs:
        total = total + held_ref[...]
    out_ref[...] = total.astype(out_ref.dtype)


def mix_second(left, part, kind=BF16, held=(), chunk=256):
    rows = left.shape[0]
    column = lambda count: pl.BlockSpec((count, chunk), lambda c: (0, c))
    return pl.pallas_call(
        second_kernel,
        grid=(WIDTH // chunk,),
        in_specs=[pl.BlockSpec(memory_space=VMEM), column(part.shape[0])]
        + [column(rows) for _ in held],
        out_specs=column(rows),
        out_shape=HBM((rows, WIDTH), kind),
        **params("mix_second"),
    )(in_vmem(left), in_vmem(part), *(in_hbm(array) for array in held))


def gelu_of_twice(v):
    inner = v * (v * v * BF16(8 * 0.7978845608028654 * 0.044715) + BF16(2 * 0.7978845608028654))
    return v + v * jnp.tanh(inner)


def channel_rows(which, arrived, rows_refs, weight_refs):
    slope_ref, shift_ref, gain_ref, up_ref, down_ref = weight_refs
    width = arrived.shape[-1]
    mixed = []
    for place in which:
        even, odd = arrived[:, 0, place // 2], arrived[:, 1, place // 2]
        low = low_half(even.shape)
        if place % 2:
            mixed.append(jnp.where(low, pltpu.roll(even, 4, 1), odd).reshape(-1, width))
        else:
            mixed.append(jnp.where(low, even, pltpu.roll(odd, 4, 1)).reshape(-1, width))
    mixed = jnp.concatenate(mixed)
    wide = jnp.concatenate([ref[...].reshape(-1, width) for ref in rows_refs]).astype(F32)
    gate = jnp.tanh(wide * (0.5 * slope_ref[...]) + 0.5 * shift_ref[...])
    residual = wide + mixed + mixed * gate
    scale = lax.rsqrt(jnp.mean(residual * residual, axis=-1, keepdims=True) + 1e-06)
    normed = (residual * scale * (0.5 * gain_ref[...])).astype(BF16)
    hidden = []
    for b in range(4):
        up = jnp.dot(normed[:, b * 256 : (b + 1) * 256], up_ref[b], preferred_element_type=F32)
        hidden.append(gelu_of_twice(up.astype(BF16)))
    out = []
    for k in range(4):
        taken = jnp.concatenate([h[:, k * 128 : (k + 1) * 128] for h in hidden], axis=1)
        down = jnp.dot(taken, down_ref[k], preferred_element_type=F32)
        out.append((residual[:, k * 256 : (k + 1) * 256] + down).astype(BF16))
    return jnp.concatenate(out, axis=1)


def arrived_tiles(returned_ref, pairs):
    width = returned_ref.shape[-1]
    return returned_ref[...].astype(F32).reshape(-1, 2, pairs, 8, width)


def relay_kernel(place, returned_ref, rows_ref, *refs):
    *weight_refs, out_ref = refs
    arrived = arrived_tiles(returned_ref, 1)
    out_ref[...] = channel_rows((place,), arrived, (rows_ref,), weight_refs)


def fixed(array):
    return pl.BlockSpec(array.shape, lambda s: (0,) * array.ndim)


def channel_relay(returned, rows, block, weights, count=128):
    first = block % 2 == 0
    steps = BLOCK // count
    returned = in_vmem(returned) if first else in_hbm(returned)
    return pl.pallas_call(
        functools.partial(relay_kernel, block % 2),
        grid=(steps,),
        in_specs=[
            pl.BlockSpec((2 * count, WIDTH), lambda s: (s, 0)),
            pl.BlockSpec((count, WIDTH), lambda s: (block * steps + s, 0)),
            *(fixed(array) for array in weights),
        ],
        out_specs=pl.BlockSpec((count, WIDTH), lambda s: (s, 0)),
        out_shape=HBM((BLOCK, WIDTH), BF16),
        **params("channel_relay"),
    )(returned, in_hbm(rows), *weights)


def last_kernel(returned_ref, *refs):
    *rest, out_ref = refs
    rows_refs, weight_refs = rest[:2], rest[2:]
    arrived = arrived_tiles(returned_ref, 2)
    out = channel_rows((0, 1, 2, 3), arrived, rows_refs, weight_refs)
    out_ref[...] = out.reshape(out_ref.shape)


def channel_last(returned, parts, weights, count=64):
    pair = pl.BlockSpec((2, count, WIDTH), lambda s: (0, s, 0))
    return pl.pallas_call(
        last_kernel,
        grid=(BLOCK // count,),
        in_specs=[
            pl.BlockSpec((4 * count, WIDTH), lambda s: (s, 0)),
            *(pair for _ in parts),
            *(fixed(array) for array in weights),
        ],
        out_specs=pl.BlockSpec((4, count, WIDTH), lambda s: (0, s, 0)),
        out_shape=HBM((4, BLOCK, WIDTH), BF16),
        **params("channel_last"),
    )(in_hbm(returned), *(in_hbm(p) for p in parts), *weights)


def exchange(rows):
    grouped = rows.reshape(DEVICES, -1, WIDTH)
    return lax.all_to_all(grouped, "seq", split_axis=0, concat_axis=0, tiled=True).reshape(
        rows.shape
    )


def shards(
    in_flight, fresh_rows, right_factor, left_factor, gate_gain, gate_bias, norm_gain, w_up, w_down
):
    section = lax.axis_index("pipe").reshape(1)
    rows, right, left = in_flight[0], right_factor[0], left_factor[0]
    weights = (gate_gain, gate_bias, norm_gain, w_up[0], w_down[0].reshape(4, 512, 256))
    route = [(n, n + 1) for n in range(lax.axis_size("pipe") - 1)]
    leaving = mix_first(right, rows)
    arrived = exchange(leaving)
    left_held, _ = lax.optimization_barrier((left, leaving))
    left_out = rows_by_output_half(left_held)
    by_output = rows_by_output(left_held)
    returned = []
    for half in range(2):
        matrix = spread(left_out[512 * half : 512 * half + 512])
        mixed = mix_second(matrix, arrived)
        returned.append(exchange(mixed))
    firsts, currents, arrivals = [], [], []
    for half in range(2):
        received = []
        for block in (2 * half, 2 * half + 1):
            out = channel_relay(returned[half], rows, block, weights)
            firsts.append(out)
            received.append(lax.ppermute(out, "pipe", route))
        leaving, current = mix_first_relayed(section, right, fresh_rows, received, half)
        currents.append(current.reshape(2, BLOCK, WIDTH))
        arrivals.append(exchange(leaving))
    first_out = jnp.concatenate(firsts)
    left_in = [spread(by_output, half) for half in range(2)]
    partial = mix_second(left_in[0], arrivals[0], F32)
    mixed = mix_second(left_in[1], arrivals[1], BF16, (partial,))
    final = exchange(mixed)
    second_out = channel_last(final, currents, weights)
    return first_out[None], second_out.reshape(1, 1024, WIDTH)


def solution(mesh):
    in_specs = (
        P("pipe", "seq", None),
        P("seq", None),
        P("pipe", "seq", None, None),
        P("pipe", "seq", None, None),
        P("pipe", None),
        P("pipe", None),
        P("pipe", None),
        P("pipe", None, None, None),
        P("pipe", None, None, None, None),
    )
    out_specs = (P("pipe", "seq", None), P("pipe", "seq", None))
    return jax.shard_map(
        shards, mesh=mesh, in_specs=in_specs, out_specs=out_specs, check_vma=False
    )
```

```python
import functools

import jax
import jax.numpy as jnp
from jax import lax
from jax.experimental import pallas as pl
from jax.experimental.pallas import tpu as pltpu
from jax.sharding import PartitionSpec as P


BLOCK = 256
WIDTH = 1024
DEVICES = 64
F32 = jnp.float32
BF16 = jnp.bfloat16
HBM = pltpu.MemorySpace.HBM
VMEM = pltpu.MemorySpace.VMEM
WHOLE = pl.BlockSpec(memory_space=VMEM)


def in_hbm(array):
    return pltpu.with_memory_space_constraint(array, HBM)


def in_vmem(array):
    return pltpu.with_memory_space_constraint(array, VMEM)


def params(name):
    return dict(
        name=name,
        compiler_params=pltpu.CompilerParams(vmem_limit_bytes=32 * 1024 * 1024),
    )


def low_half(shape):
    return lax.broadcasted_iota(jnp.int32, shape, 1) < 4


def mix_first_tiles(right_ref, load_rows, blocks):
    tiles = []
    for pair in range(blocks // 2):
        even, odd = (
            jnp.dot(right_ref[block], load_rows(block), preferred_element_type=F32).reshape(
                BLOCK // 8, 8, -1
            )
            for block in (2 * pair, 2 * pair + 1)
        )
        low = low_half(even.shape)
        tiles.append(
            (
                jnp.where(low, even, pltpu.roll(odd, 4, 1)),
                jnp.where(low, pltpu.roll(even, 4, 1), odd),
            )
        )
    ordered = [tiles[pair][parity] for parity in range(2) for pair in range(blocks // 2)]
    return jnp.stack(ordered, axis=1).reshape(blocks * BLOCK, -1)


def first_kernel(right_ref, rows_ref, out_ref):
    load = lambda block: rows_ref[pl.ds(block * BLOCK, BLOCK), :]
    tiles = mix_first_tiles(right_ref, load, 2).astype(BF16)
    out_ref[...] = tiles.reshape(out_ref.shape)


def mix_first(right, rows, chunk=512):
    count = rows.shape[0]
    out = pl.pallas_call(
        first_kernel,
        grid=(count // (2 * BLOCK), WIDTH // chunk),
        in_specs=[
            pl.BlockSpec((2, BLOCK, BLOCK), lambda h, c: (h, 0, 0)),
            pl.BlockSpec((2 * BLOCK, chunk), lambda h, c: (h, c)),
        ],
        out_specs=pl.BlockSpec((DEVICES, 1, 8, chunk), lambda h, c: (0, h, 0, c)),
        out_shape=HBM((DEVICES, count // (2 * BLOCK), 8, WIDTH), BF16),
        **params("mix_first"),
    )(in_hbm(right), in_hbm(rows))
    return out.reshape(count, WIDTH)


def relayed_kernel(half, chunk, section_ref, right_ref, fresh_ref, *refs):
    *received_refs, out_ref, current_ref, held_ref, sems = refs
    step = pl.program_id(0)
    columns = pl.ds(step * chunk, chunk)

    def fetch(n):
        place = pl.ds(n * chunk, chunk)
        source = fresh_ref.at[pl.ds(2 * half * BLOCK, 2 * BLOCK), place]
        return pltpu.make_async_copy(source, held_ref.at[n], sems.at[n])

    @pl.when(section_ref[0] == 0)
    def _():
        @pl.when(step == 0)
        def _():
            for n in range(WIDTH // chunk):
                fetch(n).start()

        fetch(step).wait()
        current_ref[...] = held_ref[step]

    @pl.when(section_ref[0] != 0)
    def _():
        for block, received_ref in enumerate(received_refs):
            current_ref[pl.ds(block * BLOCK, BLOCK), :] = received_ref[:, columns]

    load = lambda block: current_ref[pl.ds(block * BLOCK, BLOCK), :]
    out_ref[...] = mix_first_tiles(right_ref, load, 2).astype(BF16)


def mix_first_relayed(section, right, fresh, received, half, chunk=512):
    column = pl.BlockSpec((2 * BLOCK, chunk), lambda c: (0, c))
    return pl.pallas_call(
        functools.partial(relayed_kernel, half, chunk),
        grid=(WIDTH // chunk,),
        in_specs=[
            pl.BlockSpec(memory_space=pltpu.MemorySpace.SMEM),
            pl.BlockSpec((2, BLOCK, BLOCK), lambda c: (half, 0, 0)),
            pl.BlockSpec(memory_space=pl.ANY),
            *(pl.BlockSpec(memory_space=VMEM) for _ in received),
        ],
        out_specs=(column, column),
        out_shape=(HBM((2 * BLOCK, WIDTH), BF16),) * 2,
        scratch_shapes=[
            VMEM((WIDTH // chunk, 2 * BLOCK, chunk), BF16),
            pltpu.SemaphoreType.DMA((WIDTH // chunk,)),
        ],
        **params("mix_first_relayed"),
    )(section, in_hbm(right), in_hbm(fresh), *(in_vmem(part) for part in received))


def spread_kernel(half, rows_ref, out_ref):
    size = rows_ref.shape[1]
    chunk = 2 * size
    for start in range(0, out_ref.shape[1], chunk):
        column = start + lax.broadcasted_iota(jnp.int32, (size, chunk), 1)
        if half is None:
            source = column >> 2
        else:
            source = ((column >> 3) << 2) + 2 * half + ((column >> 2) & 1)
        place = jnp.where(lax.broadcasted_iota(jnp.int32, (size, chunk), 0) == source, 0.5, 0.0)
        full = jnp.dot(rows_ref[...], place.astype(BF16), preferred_element_type=F32)
        row = lax.broadcasted_iota(jnp.int32, full.shape, 0)
        offset = lax.broadcasted_iota(jnp.int32, full.shape, 1)
        kept = jnp.where((row & 3) == (offset & 3), full, 0.0)
        out_ref[:, start : start + chunk] = kept.astype(BF16)


def spread(rows, half=None):
    columns = 4 * BLOCK if half is None else 2 * BLOCK
    return pl.pallas_call(
        functools.partial(spread_kernel, half),
        out_shape=VMEM((rows.shape[0], columns), BF16),
        **params("spread"),
    )(rows)


def rows_by_output_half(left):
    split = left.reshape(4, DEVICES, 2, 2, BLOCK).transpose(2, 1, 3, 0, 4)
    return split.reshape(-1, BLOCK)


def rows_by_output(left):
    return left.transpose(1, 0, 2).reshape(-1, BLOCK)


def second_kernel(left_ref, part_ref, *refs):
    *held_refs, out_ref = refs
    total = jnp.dot(left_ref[...], part_ref[...], preferred_element_type=F32)
    for held_ref in held_refs:
        total = total + held_ref[...]
    out_ref[...] = total.astype(out_ref.dtype)


def mix_second(left, part, kind=BF16, held=(), chunk=256):
    rows = left.shape[0]
    column = lambda count: pl.BlockSpec((count, chunk), lambda c: (0, c))
    return pl.pallas_call(
        second_kernel,
        grid=(WIDTH // chunk,),
        in_specs=[pl.BlockSpec(memory_space=VMEM), column(part.shape[0])]
        + [column(rows) for _ in held],
        out_specs=column(rows),
        out_shape=HBM((rows, WIDTH), kind),
        **params("mix_second"),
    )(in_vmem(left), in_vmem(part), *(in_hbm(array) for array in held))


def gelu_of_twice(v):
    inner = v * (v * v * BF16(8 * 0.7978845608028654 * 0.044715) + BF16(2 * 0.7978845608028654))
    return v + v * jnp.tanh(inner)


def channel_rows(which, arrived, rows_refs, weight_refs):
    slope_ref, shift_ref, gain_ref, up_ref, down_ref = weight_refs
    width = arrived.shape[-1]
    mixed = []
    for place in which:
        even, odd = arrived[:, 0, place // 2], arrived[:, 1, place // 2]
        low = low_half(even.shape)
        if place % 2:
            mixed.append(jnp.where(low, pltpu.roll(even, 4, 1), odd).reshape(-1, width))
        else:
            mixed.append(jnp.where(low, even, pltpu.roll(odd, 4, 1)).reshape(-1, width))
    mixed = jnp.concatenate(mixed)
    wide = jnp.concatenate([ref[...].reshape(-1, width) for ref in rows_refs]).astype(F32)
    gate = jnp.tanh(wide * (0.5 * slope_ref[...]) + 0.5 * shift_ref[...])
    residual = wide + mixed + mixed * gate
    scale = lax.rsqrt(jnp.mean(residual * residual, axis=-1, keepdims=True) + 1e-06)
    normed = (residual * scale * (0.5 * gain_ref[...])).astype(BF16)
    hidden = []
    for b in range(4):
        up = jnp.dot(normed[:, b * 256 : (b + 1) * 256], up_ref[b], preferred_element_type=F32)
        hidden.append(gelu_of_twice(up.astype(BF16)))
    out = []
    for k in range(4):
        taken = jnp.concatenate([h[:, k * 128 : (k + 1) * 128] for h in hidden], axis=1)
        down = jnp.dot(taken, down_ref[k], preferred_element_type=F32)
        out.append((residual[:, k * 256 : (k + 1) * 256] + down).astype(BF16))
    return jnp.concatenate(out, axis=1)


def arrived_tiles(returned_ref, pairs):
    width = returned_ref.shape[-1]
    return returned_ref[...].astype(F32).reshape(-1, 2, pairs, 8, width)


def relay_kernel(place, returned_ref, rows_ref, *refs):
    *weight_refs, out_ref = refs
    arrived = arrived_tiles(returned_ref, 1)
    out_ref[...] = channel_rows((place,), arrived, (rows_ref,), weight_refs)


def channel_relay(returned, rows, block, weights, count=128):
    steps = BLOCK // count
    return pl.pallas_call(
        functools.partial(relay_kernel, block % 2),
        grid=(steps,),
        in_specs=[
            pl.BlockSpec((2 * count, WIDTH), lambda s: (s, 0)),
            pl.BlockSpec((count, WIDTH), lambda s: (block * steps + s, 0)),
            *(WHOLE for _ in weights),
        ],
        out_specs=pl.BlockSpec((count, WIDTH), lambda s: (s, 0)),
        out_shape=HBM((BLOCK, WIDTH), BF16),
        **params("channel_relay"),
    )(in_hbm(returned), in_hbm(rows), *weights)


def relay_first_kernel(start, returned_ref, head_ref, rows_ref, *refs):
    *weight_refs, out_ref, rows_buf, out_buf, sems = refs
    count = head_ref.shape[0]
    rest = pltpu.make_async_copy(
        rows_ref.at[pl.ds(start + count, count), :], rows_buf, sems.at[0]
    )
    rest.start()
    copies = []
    for n, source_ref in enumerate((head_ref, rows_buf)):
        if n:
            rest.wait()
        arrived = arrived_tiles(returned_ref.at[pl.ds(2 * n * count, 2 * count), :], 1)
        part = pl.ds(n * count, count)
        out_buf[part, :] = channel_rows((0,), arrived, (source_ref,), weight_refs)
        copy = pltpu.make_async_copy(out_buf.at[part, :], out_ref.at[part, :], sems.at[1 + n])
        copy.start()
        copies.append(copy)
    for copy in copies:
        copy.wait()


def channel_relay_first(returned, rows, block, weights, earlier, count=128):
    start = block * BLOCK
    held, *_ = lax.optimization_barrier((rows, *earlier))
    head = in_vmem(held[start : start + count])
    return pl.pallas_call(
        functools.partial(relay_first_kernel, start),
        in_specs=[WHOLE, WHOLE, pl.BlockSpec(memory_space=pl.ANY), *(WHOLE for _ in weights)],
        out_specs=pl.BlockSpec(memory_space=pl.ANY),
        out_shape=HBM((BLOCK, WIDTH), BF16),
        scratch_shapes=[
            VMEM((count, WIDTH), BF16),
            VMEM((BLOCK, WIDTH), BF16),
            pltpu.SemaphoreType.DMA((3,)),
        ],
        **params("channel_relay_first"),
    )(in_vmem(returned), head, in_hbm(rows), *weights)


def last_kernel(returned_ref, *refs):
    *rest, out_ref = refs
    rows_refs, weight_refs = rest[:2], rest[2:]
    arrived = arrived_tiles(returned_ref, 2)
    out = channel_rows((0, 1, 2, 3), arrived, rows_refs, weight_refs)
    out_ref[...] = out.reshape(out_ref.shape)


def channel_last(returned, parts, weights, count=64):
    pair = pl.BlockSpec((2, count, WIDTH), lambda s: (0, s, 0))
    return pl.pallas_call(
        last_kernel,
        grid=(BLOCK // count,),
        in_specs=[
            pl.BlockSpec((4 * count, WIDTH), lambda s: (s, 0)),
            *(pair for _ in parts),
            *(WHOLE for _ in weights),
        ],
        out_specs=pl.BlockSpec((4, count, WIDTH), lambda s: (0, s, 0)),
        out_shape=HBM((4, BLOCK, WIDTH), BF16),
        **params("channel_last"),
    )(in_hbm(returned), *(in_hbm(p) for p in parts), *weights)


def exchange(rows):
    grouped = rows.reshape(DEVICES, -1, WIDTH)
    return lax.all_to_all(grouped, "seq", split_axis=0, concat_axis=0, tiled=True).reshape(
        rows.shape
    )


def shards(
    in_flight, fresh_rows, right_factor, left_factor, gate_gain, gate_bias, norm_gain, w_up, w_down
):
    section = lax.axis_index("pipe").reshape(1)
    rows, right, left = in_flight[0], right_factor[0], left_factor[0]
    weights = (gate_gain, gate_bias, norm_gain, w_up[0], w_down[0].reshape(4, 512, 256))
    weights = tuple(in_vmem(array) for array in weights)
    sections = lax.axis_size("pipe")
    route = [(n, (n + 1) % sections) for n in range(sections)]
    leaving = mix_first(right, rows)
    arrived = exchange(leaving)
    left_held, _ = lax.optimization_barrier((left, leaving))
    left_out = rows_by_output_half(left_held)
    by_output = rows_by_output(left_held)
    returned = []
    for half in range(2):
        matrix = spread(left_out[512 * half : 512 * half + 512])
        mixed = mix_second(matrix, arrived)
        returned.append(exchange(mixed))
    firsts, currents, arrivals = [], [], []
    for half in range(2):
        received = []
        for block in (2 * half, 2 * half + 1):
            if block % 2:
                out = channel_relay(returned[half], rows, block, weights)
            else:
                out = channel_relay_first(
                    returned[half], rows, block, weights, firsts[-1:]
                )
            firsts.append(out)
            received.append(lax.ppermute(out, "pipe", route))
        leaving, current = mix_first_relayed(section, right, fresh_rows, received, half)
        currents.append(current.reshape(2, BLOCK, WIDTH))
        arrivals.append(exchange(leaving))
    first_out = jnp.concatenate(firsts)
    left_in = [spread(by_output, half) for half in range(2)]
    partial = mix_second(left_in[0], arrivals[0], F32)
    mixed = mix_second(left_in[1], arrivals[1], BF16, (partial,))
    final = exchange(mixed)
    second_out = channel_last(final, currents, weights)
    return first_out[None], second_out.reshape(1, 1024, WIDTH)


def solution(mesh):
    in_specs = (
        P("pipe", "seq", None),
        P("seq", None),
        P("pipe", "seq", None, None),
        P("pipe", "seq", None, None),
        P("pipe", None),
        P("pipe", None),
        P("pipe", None),
        P("pipe", None, None, None),
        P("pipe", None, None, None, None),
    )
    out_specs = (P("pipe", "seq", None), P("pipe", "seq", None))
    return jax.shard_map(
        shards, mesh=mesh, in_specs=in_specs, out_specs=out_specs, check_vma=False
    )
```

```python
import functools

import jax
import jax.numpy as jnp
from jax import lax
from jax.experimental import pallas as pl
from jax.experimental.pallas import tpu as pltpu
from jax.sharding import PartitionSpec as P


BLOCK = 256
WIDTH = 1024
DEVICES = 64
F32 = jnp.float32
BF16 = jnp.bfloat16
HBM = pltpu.MemorySpace.HBM
VMEM = pltpu.MemorySpace.VMEM
WHOLE = pl.BlockSpec(memory_space=VMEM)


def in_hbm(array):
    return pltpu.with_memory_space_constraint(array, HBM)


def in_vmem(array):
    return pltpu.with_memory_space_constraint(array, VMEM)


def params(name):
    return dict(
        name=name,
        compiler_params=pltpu.CompilerParams(vmem_limit_bytes=32 * 1024 * 1024),
    )


def low_half(shape):
    return lax.broadcasted_iota(jnp.int32, shape, 1) < 4


def mix_first_tiles(right_ref, load_rows, blocks):
    tiles = []
    for pair in range(blocks // 2):
        even, odd = (
            jnp.dot(right_ref[block], load_rows(block), preferred_element_type=F32).reshape(
                BLOCK // 8, 8, -1
            )
            for block in (2 * pair, 2 * pair + 1)
        )
        low = low_half(even.shape)
        tiles.append(
            (
                jnp.where(low, even, pltpu.roll(odd, 4, 1)),
                jnp.where(low, pltpu.roll(even, 4, 1), odd),
            )
        )
    ordered = [tiles[pair][parity] for parity in range(2) for pair in range(blocks // 2)]
    return jnp.stack(ordered, axis=1).reshape(blocks * BLOCK, -1)


def first_kernel(right_ref, rows_ref, out_ref):
    load = lambda block: rows_ref[pl.ds(block * BLOCK, BLOCK), :]
    tiles = mix_first_tiles(right_ref, load, 2).astype(BF16)
    out_ref[...] = tiles.reshape(out_ref.shape)


def mix_first(right, rows, chunk=1024):
    count = rows.shape[0]
    out = pl.pallas_call(
        first_kernel,
        grid=(count // (2 * BLOCK), WIDTH // chunk),
        in_specs=[
            pl.BlockSpec((2, BLOCK, BLOCK), lambda h, c: (h, 0, 0)),
            pl.BlockSpec((2 * BLOCK, chunk), lambda h, c: (h, c)),
        ],
        out_specs=pl.BlockSpec((DEVICES, 1, 8, chunk), lambda h, c: (0, h, 0, c)),
        out_shape=HBM((DEVICES, count // (2 * BLOCK), 8, WIDTH), BF16),
        **params("mix_first"),
    )(in_hbm(right), in_hbm(rows))
    return out.reshape(count, WIDTH)


def relayed_kernel(half, chunk, section_ref, right_ref, fresh_ref, *refs):
    *received_refs, out_ref, current_ref, held_ref, sems = refs
    step = pl.program_id(0)
    columns = pl.ds(step * chunk, chunk)

    def fetch(n):
        place = pl.ds(n * chunk, chunk)
        source = fresh_ref.at[pl.ds(2 * half * BLOCK, 2 * BLOCK), place]
        return pltpu.make_async_copy(source, held_ref.at[n], sems.at[n])

    @pl.when(section_ref[0] == 0)
    def _():
        @pl.when(step == 0)
        def _():
            for n in range(WIDTH // chunk):
                fetch(n).start()

        fetch(step).wait()
        current_ref[...] = held_ref[step]

    @pl.when(section_ref[0] != 0)
    def _():
        for block, received_ref in enumerate(received_refs):
            current_ref[pl.ds(block * BLOCK, BLOCK), :] = received_ref[:, columns]

    load = lambda block: current_ref[pl.ds(block * BLOCK, BLOCK), :]
    out_ref[...] = mix_first_tiles(right_ref, load, 2).astype(BF16)


def mix_first_relayed(section, right, fresh, received, half, chunk=512):
    column = pl.BlockSpec((2 * BLOCK, chunk), lambda c: (0, c))
    return pl.pallas_call(
        functools.partial(relayed_kernel, half, chunk),
        grid=(WIDTH // chunk,),
        in_specs=[
            pl.BlockSpec(memory_space=pltpu.MemorySpace.SMEM),
            pl.BlockSpec((2, BLOCK, BLOCK), lambda c: (half, 0, 0)),
            pl.BlockSpec(memory_space=pl.ANY),
            *(pl.BlockSpec(memory_space=VMEM) for _ in received),
        ],
        out_specs=(column, column),
        out_shape=(HBM((2 * BLOCK, WIDTH), BF16),) * 2,
        scratch_shapes=[
            VMEM((WIDTH // chunk, 2 * BLOCK, chunk), BF16),
            pltpu.SemaphoreType.DMA((WIDTH // chunk,)),
        ],
        **params("mix_first_relayed"),
    )(section, in_hbm(right), in_hbm(fresh), *(in_vmem(part) for part in received))


def spread_kernel(half, rows_ref, out_ref):
    size = rows_ref.shape[1]
    chunk = 2 * size
    for start in range(0, out_ref.shape[1], chunk):
        column = start + lax.broadcasted_iota(jnp.int32, (size, chunk), 1)
        if half is None:
            source = column >> 2
        else:
            source = ((column >> 3) << 2) + 2 * half + ((column >> 2) & 1)
        place = jnp.where(lax.broadcasted_iota(jnp.int32, (size, chunk), 0) == source, 0.5, 0.0)
        full = jnp.dot(rows_ref[...], place.astype(BF16), preferred_element_type=F32)
        row = lax.broadcasted_iota(jnp.int32, full.shape, 0)
        offset = lax.broadcasted_iota(jnp.int32, full.shape, 1)
        kept = jnp.where((row & 3) == (offset & 3), full, 0.0)
        out_ref[:, start : start + chunk] = kept.astype(BF16)


def spread(rows, half=None):
    columns = 4 * BLOCK if half is None else 2 * BLOCK
    return pl.pallas_call(
        functools.partial(spread_kernel, half),
        out_shape=VMEM((rows.shape[0], columns), BF16),
        **params("spread"),
    )(rows)


def rows_by_output_half(left):
    split = left.reshape(4, DEVICES, 2, 2, BLOCK).transpose(2, 1, 3, 0, 4)
    return split.reshape(-1, BLOCK)


def rows_by_output(left):
    return left.transpose(1, 0, 2).reshape(-1, BLOCK)


def second_kernel(left_ref, part_ref, *refs):
    *held_refs, out_ref = refs
    total = jnp.dot(left_ref[...], part_ref[...], preferred_element_type=F32)
    for held_ref in held_refs:
        total = total + held_ref[...]
    out_ref[...] = total.astype(out_ref.dtype)


def mix_second(left, part, kind=BF16, held=(), chunk=WIDTH):
    rows = left.shape[0]
    column = lambda count: pl.BlockSpec((count, chunk), lambda c: (0, c))
    return pl.pallas_call(
        second_kernel,
        grid=(WIDTH // chunk,),
        in_specs=[pl.BlockSpec(memory_space=VMEM), column(part.shape[0])]
        + [column(rows) for _ in held],
        out_specs=column(rows),
        out_shape=HBM((rows, WIDTH), kind),
        **params("mix_second"),
    )(in_vmem(left), in_vmem(part), *(in_hbm(array) for array in held))


def gelu_of_twice(v):
    inner = v * (v * v * BF16(8 * 0.7978845608028654 * 0.044715) + BF16(2 * 0.7978845608028654))
    return v + v * jnp.tanh(inner)


def gated_rows(which, arrived, rows_refs, weight_refs):
    slope_ref, shift_ref, gain_ref, *_ = weight_refs
    width = arrived.shape[-1]
    mixed = []
    for place in which:
        even, odd = arrived[:, 0, place // 2], arrived[:, 1, place // 2]
        low = low_half(even.shape)
        if place % 2:
            mixed.append(jnp.where(low, pltpu.roll(even, 4, 1), odd).reshape(-1, width))
        else:
            mixed.append(jnp.where(low, even, pltpu.roll(odd, 4, 1)).reshape(-1, width))
    mixed = jnp.concatenate(mixed)
    wide = jnp.concatenate([ref[...].reshape(-1, width) for ref in rows_refs]).astype(F32)
    gate = jnp.tanh(wide * (0.5 * slope_ref[...]) + 0.5 * shift_ref[...])
    residual = wide + mixed + mixed * gate
    scale = lax.rsqrt(jnp.mean(residual * residual, axis=-1, keepdims=True) + 1e-06)
    return residual, (residual * scale * (0.5 * gain_ref[...])).astype(BF16)


def mlp_columns(residual, normed, weight_refs):
    *_, up_ref, down_ref = weight_refs
    hidden = []
    for b in range(4):
        up = jnp.dot(normed[:, b * 256 : (b + 1) * 256], up_ref[b], preferred_element_type=F32)
        hidden.append(gelu_of_twice(up.astype(BF16)))
    for k in range(4):
        taken = jnp.concatenate([h[:, k * 128 : (k + 1) * 128] for h in hidden], axis=1)
        down = jnp.dot(taken, down_ref[k], preferred_element_type=F32)
        yield (residual[:, k * 256 : (k + 1) * 256] + down).astype(BF16)


def channel_rows(which, arrived, rows_refs, weight_refs):
    residual, normed = gated_rows(which, arrived, rows_refs, weight_refs)
    return jnp.concatenate(list(mlp_columns(residual, normed, weight_refs)), axis=1)


def arrived_tiles(returned_ref, pairs):
    width = returned_ref.shape[-1]
    return returned_ref[...].astype(F32).reshape(-1, 2, pairs, 8, width)


def relay_kernel(place, returned_ref, rows_ref, *refs):
    *weight_refs, out_ref = refs
    arrived = arrived_tiles(returned_ref, 1)
    out_ref[...] = channel_rows((place,), arrived, (rows_ref,), weight_refs)


def channel_relay(returned, rows, block, weights, count=128):
    steps = BLOCK // count
    return pl.pallas_call(
        functools.partial(relay_kernel, block % 2),
        grid=(steps,),
        in_specs=[
            pl.BlockSpec((2 * count, WIDTH), lambda s: (s, 0)),
            pl.BlockSpec((count, WIDTH), lambda s: (block * steps + s, 0)),
            *(WHOLE for _ in weights),
        ],
        out_specs=pl.BlockSpec((count, WIDTH), lambda s: (s, 0)),
        out_shape=HBM((BLOCK, WIDTH), BF16),
        **params("channel_relay"),
    )(in_hbm(returned), in_hbm(rows), *weights)


def relay_first_kernel(start, returned_ref, head_ref, rows_ref, *refs):
    *weight_refs, out_ref, rows_buf, out_buf, sems = refs
    held, count = head_ref.shape[0], rows_buf.shape[0]
    rest = pltpu.make_async_copy(
        rows_ref.at[pl.ds(start + held, count), :], rows_buf, sems.at[0]
    )
    rest.start()
    first = arrived_tiles(returned_ref.at[pl.ds(0, 2 * held), :], 1)
    pieces = [gated_rows((0,), first, (head_ref,), weight_refs)]
    rest.wait()
    second = arrived_tiles(returned_ref.at[pl.ds(2 * held, 2 * count), :], 1)
    pieces.append(gated_rows((0,), second, (rows_buf,), weight_refs))
    residual, normed = (jnp.concatenate(piece) for piece in zip(*pieces))
    copies = []
    for k, out in enumerate(mlp_columns(residual, normed, weight_refs)):
        part = pl.ds(k * 256, 256)
        out_buf[:, part] = out
        if k % 2:
            part = pl.ds((k - 1) * 256, 512)
            sem = sems.at[1 + k // 2]
            copy = pltpu.make_async_copy(out_buf.at[:, part], out_ref.at[:, part], sem)
            copy.start()
            copies.append(copy)
    for copy in copies:
        copy.wait()


def channel_relay_first(returned, rows, block, weights, earlier, held=192):
    start = block * BLOCK
    source, *_ = lax.optimization_barrier((rows, *earlier))
    head = in_vmem(source[start : start + held])
    return pl.pallas_call(
        functools.partial(relay_first_kernel, start),
        in_specs=[WHOLE, WHOLE, pl.BlockSpec(memory_space=pl.ANY), *(WHOLE for _ in weights)],
        out_specs=pl.BlockSpec(memory_space=pl.ANY),
        out_shape=HBM((BLOCK, WIDTH), BF16),
        scratch_shapes=[
            VMEM((BLOCK - held, WIDTH), BF16),
            VMEM((BLOCK, WIDTH), BF16),
            pltpu.SemaphoreType.DMA((3,)),
        ],
        **params("channel_relay_first"),
    )(in_vmem(returned), head, in_hbm(rows), *weights)


def last_kernel(returned_ref, *refs):
    *rest, out_ref = refs
    rows_refs, weight_refs = rest[:2], rest[2:]
    arrived = arrived_tiles(returned_ref, 2)
    out = channel_rows((0, 1, 2, 3), arrived, rows_refs, weight_refs)
    out_ref[...] = out.reshape(out_ref.shape)


def channel_last(returned, parts, weights, count=64):
    pair = pl.BlockSpec((2, count, WIDTH), lambda s: (0, s, 0))
    return pl.pallas_call(
        last_kernel,
        grid=(BLOCK // count,),
        in_specs=[
            pl.BlockSpec((4 * count, WIDTH), lambda s: (s, 0)),
            *(pair for _ in parts),
            *(WHOLE for _ in weights),
        ],
        out_specs=pl.BlockSpec((4, count, WIDTH), lambda s: (0, s, 0)),
        out_shape=HBM((4, BLOCK, WIDTH), BF16),
        **params("channel_last"),
    )(in_hbm(returned), *(in_hbm(p) for p in parts), *weights)


def exchange(rows):
    grouped = rows.reshape(DEVICES, -1, WIDTH)
    return lax.all_to_all(grouped, "seq", split_axis=0, concat_axis=0, tiled=True).reshape(
        rows.shape
    )


def shards(
    in_flight, fresh_rows, right_factor, left_factor, gate_gain, gate_bias, norm_gain, w_up, w_down
):
    section = lax.axis_index("pipe").reshape(1)
    rows, right, left = in_flight[0], right_factor[0], left_factor[0]
    weights = (gate_gain, gate_bias, norm_gain, w_up[0], w_down[0].reshape(4, 512, 256))
    weights = tuple(in_vmem(array) for array in weights)
    sections = lax.axis_size("pipe")
    route = [(n, (n + 1) % sections) for n in range(sections)]
    leaving = mix_first(right, rows)
    arrived = exchange(leaving)
    left_held, _ = lax.optimization_barrier((left, leaving))
    left_out = rows_by_output_half(left_held)
    by_output = rows_by_output(left_held)
    returned = []
    for half in range(2):
        matrix = spread(left_out[512 * half : 512 * half + 512])
        mixed = mix_second(matrix, arrived)
        returned.append(exchange(mixed))
    firsts, currents, arrivals = [], [], []
    for half in range(2):
        received = []
        for block in (2 * half, 2 * half + 1):
            if block % 2:
                out = channel_relay(returned[half], rows, block, weights)
            else:
                out = channel_relay_first(
                    returned[half], rows, block, weights, firsts[-1:]
                )
            firsts.append(out)
            received.append(lax.ppermute(out, "pipe", route))
        leaving, current = mix_first_relayed(section, right, fresh_rows, received, half)
        currents.append(current.reshape(2, BLOCK, WIDTH))
        arrivals.append(exchange(leaving))
    first_out = jnp.concatenate(firsts)
    left_in = [spread(by_output, half) for half in range(2)]
    partial = mix_second(left_in[0], arrivals[0], F32, (), 512)
    mixed = mix_second(left_in[1], arrivals[1], BF16, (partial,), 512)
    final = exchange(mixed)
    second_out = channel_last(final, currents, weights)
    return first_out[None], second_out.reshape(1, 1024, WIDTH)


def solution(mesh):
    in_specs = (
        P("pipe", "seq", None),
        P("seq", None),
        P("pipe", "seq", None, None),
        P("pipe", "seq", None, None),
        P("pipe", None),
        P("pipe", None),
        P("pipe", None),
        P("pipe", None, None, None),
        P("pipe", None, None, None, None),
    )
    out_specs = (P("pipe", "seq", None), P("pipe", "seq", None))
    return jax.shard_map(
        shards, mesh=mesh, in_specs=in_specs, out_specs=out_specs, check_vma=False
    )
```

```python
import functools

import jax
import jax.numpy as jnp
from jax import lax
from jax.experimental import pallas as pl
from jax.experimental.pallas import tpu as pltpu
from jax.sharding import PartitionSpec as P


BLOCK = 256
WIDTH = 1024
DEVICES = 64
F32 = jnp.float32
BF16 = jnp.bfloat16
HBM = pltpu.MemorySpace.HBM
VMEM = pltpu.MemorySpace.VMEM
WHOLE = pl.BlockSpec(memory_space=VMEM)


def in_hbm(array):
    return pltpu.with_memory_space_constraint(array, HBM)


def in_vmem(array):
    return pltpu.with_memory_space_constraint(array, VMEM)


def params(name):
    return dict(
        name=name,
        compiler_params=pltpu.CompilerParams(vmem_limit_bytes=32 * 1024 * 1024),
    )


def low_half(shape):
    return lax.broadcasted_iota(jnp.int32, shape, 1) < 4


def mix_first_tiles(right_ref, load_rows, blocks):
    tiles = []
    for pair in range(blocks // 2):
        even, odd = (
            jnp.dot(right_ref[block], load_rows(block), preferred_element_type=F32).reshape(
                BLOCK // 8, 8, -1
            )
            for block in (2 * pair, 2 * pair + 1)
        )
        low = low_half(even.shape)
        tiles.append(
            (
                jnp.where(low, even, pltpu.roll(odd, 4, 1)),
                jnp.where(low, pltpu.roll(even, 4, 1), odd),
            )
        )
    ordered = [tiles[pair][parity] for parity in range(2) for pair in range(blocks // 2)]
    return jnp.stack(ordered, axis=1).reshape(blocks * BLOCK, -1)


def first_kernel(right_ref, rows_ref, out_ref):
    load = lambda block: rows_ref[pl.ds(block * BLOCK, BLOCK), :]
    tiles = mix_first_tiles(right_ref, load, 2).astype(BF16)
    out_ref[...] = tiles.reshape(out_ref.shape)


def mix_first(right, rows, chunk=1024):
    count = rows.shape[0]
    out = pl.pallas_call(
        first_kernel,
        grid=(count // (2 * BLOCK), WIDTH // chunk),
        in_specs=[
            pl.BlockSpec((2, BLOCK, BLOCK), lambda h, c: (h, 0, 0)),
            pl.BlockSpec((2 * BLOCK, chunk), lambda h, c: (h, c)),
        ],
        out_specs=pl.BlockSpec((DEVICES, 1, 8, chunk), lambda h, c: (0, h, 0, c)),
        out_shape=HBM((DEVICES, count // (2 * BLOCK), 8, WIDTH), BF16),
        **params("mix_first"),
    )(in_hbm(right), in_hbm(rows))
    return out.reshape(count, WIDTH)


def relayed_kernel(half, chunk, section_ref, right_ref, fresh_ref, *refs):
    *received_refs, out_ref, current_ref, held_ref, sems = refs
    step = pl.program_id(0)
    columns = pl.ds(step * chunk, chunk)

    def fetch(n):
        place = pl.ds(n * chunk, chunk)
        source = fresh_ref.at[pl.ds(2 * half * BLOCK, 2 * BLOCK), place]
        return pltpu.make_async_copy(source, held_ref.at[n], sems.at[n])

    @pl.when(section_ref[0] == 0)
    def _():
        @pl.when(step == 0)
        def _():
            for n in range(WIDTH // chunk):
                fetch(n).start()

        fetch(step).wait()
        current_ref[...] = held_ref[step]

    @pl.when(section_ref[0] != 0)
    def _():
        for block, received_ref in enumerate(received_refs):
            current_ref[pl.ds(block * BLOCK, BLOCK), :] = received_ref[:, columns]

    load = lambda block: current_ref[pl.ds(block * BLOCK, BLOCK), :]
    out_ref[...] = mix_first_tiles(right_ref, load, 2).astype(BF16)


def mix_first_relayed(section, right, fresh, received, half, chunk=512):
    column = pl.BlockSpec((2 * BLOCK, chunk), lambda c: (0, c))
    return pl.pallas_call(
        functools.partial(relayed_kernel, half, chunk),
        grid=(WIDTH // chunk,),
        in_specs=[
            pl.BlockSpec(memory_space=pltpu.MemorySpace.SMEM),
            pl.BlockSpec((2, BLOCK, BLOCK), lambda c: (half, 0, 0)),
            pl.BlockSpec(memory_space=pl.ANY),
            *(pl.BlockSpec(memory_space=VMEM) for _ in received),
        ],
        out_specs=(column, column),
        out_shape=(HBM((2 * BLOCK, WIDTH), BF16),) * 2,
        scratch_shapes=[
            VMEM((WIDTH // chunk, 2 * BLOCK, chunk), BF16),
            pltpu.SemaphoreType.DMA((WIDTH // chunk,)),
        ],
        **params("mix_first_relayed"),
    )(section, in_hbm(right), in_hbm(fresh), *(in_vmem(part) for part in received))


def spread_kernel(half, rows_ref, out_ref):
    size = rows_ref.shape[1]
    chunk = 2 * size
    for start in range(0, out_ref.shape[1], chunk):
        column = start + lax.broadcasted_iota(jnp.int32, (size, chunk), 1)
        if half is None:
            source = column >> 2
        else:
            source = ((column >> 3) << 2) + 2 * half + ((column >> 2) & 1)
        place = jnp.where(lax.broadcasted_iota(jnp.int32, (size, chunk), 0) == source, 0.5, 0.0)
        full = jnp.dot(rows_ref[...], place.astype(BF16), preferred_element_type=F32)
        row = lax.broadcasted_iota(jnp.int32, full.shape, 0)
        offset = lax.broadcasted_iota(jnp.int32, full.shape, 1)
        kept = jnp.where((row & 3) == (offset & 3), full, 0.0)
        out_ref[:, start : start + chunk] = kept.astype(BF16)


def spread(rows, half=None):
    columns = 4 * BLOCK if half is None else 2 * BLOCK
    return pl.pallas_call(
        functools.partial(spread_kernel, half),
        out_shape=VMEM((rows.shape[0], columns), BF16),
        **params("spread"),
    )(rows)


def rows_by_output_half(left):
    split = left.reshape(4, DEVICES, 2, 2, BLOCK).transpose(2, 1, 3, 0, 4)
    return split.reshape(-1, BLOCK)


def rows_by_output(left):
    return left.transpose(1, 0, 2).reshape(-1, BLOCK)


def second_kernel(left_ref, part_ref, *refs):
    *held_refs, out_ref = refs
    total = jnp.dot(left_ref[...], part_ref[...], preferred_element_type=F32)
    for held_ref in held_refs:
        total = total + held_ref[...]
    out_ref[...] = total.astype(out_ref.dtype)


def mix_second(left, part, kind=BF16, held=(), chunk=WIDTH):
    rows = left.shape[0]
    column = lambda count: pl.BlockSpec((count, chunk), lambda c: (0, c))
    return pl.pallas_call(
        second_kernel,
        grid=(WIDTH // chunk,),
        in_specs=[pl.BlockSpec(memory_space=VMEM), column(part.shape[0])]
        + [column(rows) for _ in held],
        out_specs=column(rows),
        out_shape=HBM((rows, WIDTH), kind),
        **params("mix_second"),
    )(in_vmem(left), in_vmem(part), *(in_hbm(array) for array in held))


def gelu_of_twice(v):
    inner = v * (v * v * BF16(8 * 0.7978845608028654 * 0.044715) + BF16(2 * 0.7978845608028654))
    return v + v * jnp.tanh(inner)


def gated_rows(which, arrived, rows_refs, weight_refs):
    slope_ref, shift_ref, gain_ref, *_ = weight_refs
    width = arrived.shape[-1]
    mixed = []
    for place in which:
        even, odd = arrived[:, 0, place // 2], arrived[:, 1, place // 2]
        low = low_half(even.shape)
        if place % 2:
            mixed.append(jnp.where(low, pltpu.roll(even, 4, 1), odd).reshape(-1, width))
        else:
            mixed.append(jnp.where(low, even, pltpu.roll(odd, 4, 1)).reshape(-1, width))
    mixed = jnp.concatenate(mixed)
    wide = jnp.concatenate([ref[...].reshape(-1, width) for ref in rows_refs]).astype(F32)
    gate = jnp.tanh(wide * (0.5 * slope_ref[...]) + 0.5 * shift_ref[...])
    residual = wide + mixed + mixed * gate
    scale = lax.rsqrt(jnp.mean(residual * residual, axis=-1, keepdims=True) + 1e-06)
    return residual, (residual * scale * (0.5 * gain_ref[...])).astype(BF16)


def mlp_columns(residual, normed, weight_refs):
    *_, up_ref, down_ref = weight_refs
    hidden = []
    for b in range(4):
        up = jnp.dot(normed[:, b * 256 : (b + 1) * 256], up_ref[b], preferred_element_type=F32)
        hidden.append(gelu_of_twice(up.astype(BF16)))
    for k in range(4):
        taken = jnp.concatenate([h[:, k * 128 : (k + 1) * 128] for h in hidden], axis=1)
        down = jnp.dot(taken, down_ref[k], preferred_element_type=F32)
        yield (residual[:, k * 256 : (k + 1) * 256] + down).astype(BF16)


def channel_rows(which, arrived, rows_refs, weight_refs):
    residual, normed = gated_rows(which, arrived, rows_refs, weight_refs)
    return jnp.concatenate(list(mlp_columns(residual, normed, weight_refs)), axis=1)


def arrived_tiles(returned_ref, pairs):
    width = returned_ref.shape[-1]
    return returned_ref[...].astype(F32).reshape(-1, 2, pairs, 8, width)


def relay_kernel(place, returned_ref, rows_ref, *refs):
    *weight_refs, out_ref = refs
    arrived = arrived_tiles(returned_ref, 1)
    out_ref[...] = channel_rows((place,), arrived, (rows_ref,), weight_refs)


def channel_relay(returned, rows, block, weights, count=128):
    steps = BLOCK // count
    return pl.pallas_call(
        functools.partial(relay_kernel, block % 2),
        grid=(steps,),
        in_specs=[
            pl.BlockSpec((2 * count, WIDTH), lambda s: (s, 0)),
            pl.BlockSpec((count, WIDTH), lambda s: (block * steps + s, 0)),
            *(WHOLE for _ in weights),
        ],
        out_specs=pl.BlockSpec((count, WIDTH), lambda s: (s, 0)),
        out_shape=HBM((BLOCK, WIDTH), BF16),
        **params("channel_relay"),
    )(in_hbm(returned), in_hbm(rows), *weights)


def relay_first_kernel(start, returned_ref, head_ref, rows_ref, *refs):
    *weight_refs, out_ref, rows_buf, out_buf, sems = refs
    held, count = head_ref.shape[0], rows_buf.shape[0]
    rest = pltpu.make_async_copy(
        rows_ref.at[pl.ds(start + held, count), :], rows_buf, sems.at[0]
    )
    rest.start()
    first = arrived_tiles(returned_ref.at[pl.ds(0, 2 * held), :], 1)
    pieces = [gated_rows((0,), first, (head_ref,), weight_refs)]
    rest.wait()
    second = arrived_tiles(returned_ref.at[pl.ds(2 * held, 2 * count), :], 1)
    pieces.append(gated_rows((0,), second, (rows_buf,), weight_refs))
    residual, normed = (jnp.concatenate(piece) for piece in zip(*pieces))
    copies = []
    for k, out in enumerate(mlp_columns(residual, normed, weight_refs)):
        part = pl.ds(k * 256, 256)
        out_buf[:, part] = out
        if k % 2:
            part = pl.ds((k - 1) * 256, 512)
            sem = sems.at[1 + k // 2]
            copy = pltpu.make_async_copy(out_buf.at[:, part], out_ref.at[:, part], sem)
            copy.start()
            copies.append(copy)
    for copy in copies:
        copy.wait()


def channel_relay_first(returned, rows, block, weights, earlier, held=192):
    start = block * BLOCK
    source, *_ = lax.optimization_barrier((rows, *earlier))
    head = in_vmem(source[start : start + held])
    return pl.pallas_call(
        functools.partial(relay_first_kernel, start),
        in_specs=[WHOLE, WHOLE, pl.BlockSpec(memory_space=pl.ANY), *(WHOLE for _ in weights)],
        out_specs=pl.BlockSpec(memory_space=pl.ANY),
        out_shape=HBM((BLOCK, WIDTH), BF16),
        scratch_shapes=[
            VMEM((BLOCK - held, WIDTH), BF16),
            VMEM((BLOCK, WIDTH), BF16),
            pltpu.SemaphoreType.DMA((3,)),
        ],
        **params("channel_relay_first"),
    )(in_vmem(returned), head, in_hbm(rows), *weights)


def last_kernel(counts, returned_ref, *refs):
    parts_refs, weight_refs, out_ref = refs[:2], refs[2:7], refs[7]
    returned_buf, rows_buf, out_buf, sems, out_sems = refs[8:]
    starts = [sum(counts[:n]) for n in range(len(counts))]
    arriving = []
    for n, (start, count) in enumerate(zip(starts, counts)):
        taken = pl.ds(4 * start, 4 * count)
        copies = [
            pltpu.make_async_copy(
                returned_ref.at[taken, :], returned_buf.at[taken, :], sems.at[n, 0]
            )
        ]
        for half, part_ref in enumerate(parts_refs):
            place = pl.ds(start, count)
            copies.append(
                pltpu.make_async_copy(
                    part_ref.at[:, place, :],
                    rows_buf.at[pl.ds(2 * half, 2), place, :],
                    sems.at[n, 1 + half],
                )
            )
        for copy in copies:
            copy.start()
        arriving.append(copies)
    leaving = []
    for n, (start, count) in enumerate(zip(starts, counts)):
        for copy in arriving[n]:
            copy.wait()
        place = pl.ds(start, count)
        arrived = arrived_tiles(returned_buf.at[pl.ds(4 * start, 4 * count), :], 2)
        rows_refs = (rows_buf.at[:, place, :],)
        out = channel_rows((0, 1, 2, 3), arrived, rows_refs, weight_refs)
        out_buf[:, place, :] = out.reshape(4, count, WIDTH)
        copy = pltpu.make_async_copy(
            out_buf.at[:, place, :], out_ref.at[:, place, :], out_sems.at[n]
        )
        copy.start()
        leaving.append(copy)
    for copy in leaving:
        copy.wait()


def channel_last(returned, parts, weights, counts=(64, 128, 64)):
    anywhere = pl.BlockSpec(memory_space=pl.ANY)
    return pl.pallas_call(
        functools.partial(last_kernel, counts),
        in_specs=[anywhere, *(anywhere for _ in parts), *(WHOLE for _ in weights)],
        out_specs=anywhere,
        out_shape=HBM((4, BLOCK, WIDTH), BF16),
        scratch_shapes=[
            VMEM((4 * BLOCK, WIDTH), BF16),
            VMEM((4, BLOCK, WIDTH), BF16),
            VMEM((4, BLOCK, WIDTH), BF16),
            pltpu.SemaphoreType.DMA((len(counts), 3)),
            pltpu.SemaphoreType.DMA((len(counts),)),
        ],
        **params("channel_last"),
    )(in_hbm(returned), *(in_hbm(part) for part in parts), *weights)


def exchange(rows):
    grouped = rows.reshape(DEVICES, -1, WIDTH)
    return lax.all_to_all(grouped, "seq", split_axis=0, concat_axis=0, tiled=True).reshape(
        rows.shape
    )


def shards(
    in_flight, fresh_rows, right_factor, left_factor, gate_gain, gate_bias, norm_gain, w_up, w_down
):
    section = lax.axis_index("pipe").reshape(1)
    rows, right, left = in_flight[0], right_factor[0], left_factor[0]
    weights = (gate_gain, gate_bias, norm_gain, w_up[0], w_down[0].reshape(4, 512, 256))
    weights = tuple(in_vmem(array) for array in weights)
    sections = lax.axis_size("pipe")
    route = [(n, (n + 1) % sections) for n in range(sections)]
    leaving = mix_first(right, rows)
    arrived = exchange(leaving)
    left_held, _ = lax.optimization_barrier((left, leaving))
    left_out = rows_by_output_half(left_held)
    by_output = rows_by_output(left_held)
    returned = []
    for half in range(2):
        matrix = spread(left_out[512 * half : 512 * half + 512])
        mixed = mix_second(matrix, arrived)
        returned.append(exchange(mixed))
    firsts, currents, arrivals = [], [], []
    for half in range(2):
        received = []
        for block in (2 * half, 2 * half + 1):
            if block % 2:
                out = channel_relay(returned[half], rows, block, weights)
            else:
                out = channel_relay_first(
                    returned[half], rows, block, weights, firsts[-1:]
                )
            firsts.append(out)
            received.append(lax.ppermute(out, "pipe", route))
        leaving, current = mix_first_relayed(section, right, fresh_rows, received, half)
        currents.append(current.reshape(2, BLOCK, WIDTH))
        arrivals.append(exchange(leaving))
    first_out = jnp.concatenate(firsts)
    left_in = [spread(by_output, half) for half in range(2)]
    partial = mix_second(left_in[0], arrivals[0], F32, (), 512)
    mixed = mix_second(left_in[1], arrivals[1], BF16, (partial,), 512)
    final = exchange(mixed)
    second_out = channel_last(final, currents, weights)
    return first_out[None], second_out.reshape(1, 1024, WIDTH)


def solution(mesh):
    in_specs = (
        P("pipe", "seq", None),
        P("seq", None),
        P("pipe", "seq", None, None),
        P("pipe", "seq", None, None),
        P("pipe", None),
        P("pipe", None),
        P("pipe", None),
        P("pipe", None, None, None),
        P("pipe", None, None, None, None),
    )
    out_specs = (P("pipe", "seq", None), P("pipe", "seq", None))
    return jax.shard_map(
        shards, mesh=mesh, in_specs=in_specs, out_specs=out_specs, check_vma=False
    )
```
